32 devices in a mesh: tm: 4 (over y, x), dp: 8 (over z, core).
Axes of the slice: x: 2, y: 2, z: 4, core: 2. Of those that a mesh axis runs over, the one named last changes fastest.
Arguments:
- video_clips: bfloat16 [8, 8, 16, 16, 256], P('dp', 'tm'), may hold values from -6 to 6
- cotangent: bfloat16 [8, 8, 16, 16, 256], P('dp', 'tm'), may hold values from -6 to 6
- weight: bfloat16 [3, 3, 3, 256, 256], replicated, may hold values from -0.078125 to 0.078125
- lengths: int32 [8], P('dp'), may hold values from 1 to 8, as said below
Outputs:
- conv_out: bfloat16 [8, 8, 16, 16, 256], P('dp', 'tm')
- input_grad: bfloat16 [8, 8, 16, 16, 256], P('dp', 'tm')
- weight_grad: float32 [3, 3, 3, 256, 256], P(None, None, None, 'dp')
The draws below stay inside these ranges and needn't reach their ends.
Inputs may be any that keep to these rules, and one draw needn't show every extreme that they name: `lengths`: some clip has 8 frames and some clip has one frame.
All inputs are finite; a program needn't handle non-finite values.
Results may differ from the reference program's by a relative error of at most 0.0048.
Values may be sent and summed in bfloat16 or wider, within the bound.
No kernel may reach another device: no remote copies, remote signals or barrier semaphores. Data moves between devices by JAX's collectives and lax.ppermute only.
A program may use at most 128 MiB of HBM per device.

```python
import jax
import jax.numpy as jnp
from jax import lax

CHANNELS = 256
HEIGHT = 16
WIDTH = 16
FRAMES = 8
CLIPS = 8


def draw_lengths(key, part):
    first_key, second_key = jax.random.split(jax.random.fold_in(key, 17))
    drawn = jax.random.randint(first_key, (CLIPS,), 1, FRAMES + 1)
    order = jax.random.permutation(second_key, CLIPS)
    drawn = drawn.at[order[0]].set(FRAMES)
    drawn = drawn.at[order[1]].set(1)
    return drawn.astype(jnp.int32)


def spiked(result, key, source, target, shards_of, factor):
    owner, partner = [(jnp.arange(result.shape[axis_at]) // (result.shape[axis_at] // shards_of)).reshape([-1 if axis == axis_at else 1 for axis in range(result.ndim)]) for axis_at in (source, target)]
    chosen = jax.random.permutation(key, shards_of)[partner]
    strong = (owner == chosen) | (owner == (partner + shards_of // 2) % shards_of)
    return jnp.where(strong, factor * result, result)


def level_of(stream_key, dims, shards, smallest, largest):
    loudness, own = 1.0, jax.random.fold_in(stream_key, 6)
    for axis_at, parts in shards:
        draws = jnp.exp(jax.random.uniform(jax.random.fold_in(own, axis_at), (parts,), jnp.float32, smallest / len(shards), largest / len(shards)))
        loudness = loudness * jnp.repeat(draws, dims[axis_at] // parts).reshape([-1 if axis == axis_at else 1 for axis in range(len(dims))])
    return loudness


def noise(own_key, shape, spread, limit, cuts=(), held_as=jnp.bfloat16):
    values = jax.random.normal(own_key, shape, jnp.float32) * spread
    if len(cuts) > 0:
        values = level_of(own_key, shape, cuts, -0.22, 0.18) * values
    return jnp.clip(values, min=-limit, max=limit).astype(held_as)


def gaussian_with(key, extent, width, reach, cuts, heavy, held_as=jnp.bfloat16):
    result = width * jax.random.normal(key, extent, jnp.float32)
    if cuts:
        result = result * level_of(key, extent, cuts, -0.22, 0.18)
    return jnp.clip(spiked(result, jax.random.fold_in(key, 3), *heavy), -reach, reach).astype(held_as)


def setup_inputs(seed: int = 0) -> dict:
    seeds = jax.random.split(jax.random.key(seed), 5)
    video_clips = gaussian_with(seeds[0], (CLIPS, FRAMES, HEIGHT, WIDTH, CHANNELS), 1.0, 6.0, ((0, 8), (1, 4)), (0, 4, 8, 2.0))
    cotangent = noise(seeds[1], (CLIPS, FRAMES, HEIGHT, WIDTH, CHANNELS), 1.0, 6.0, ((0, 8), (1, 4)))
    weight = noise(seeds[2], (3, 3, 3, CHANNELS, CHANNELS), (27 * CHANNELS) ** -0.5, 0.078125)
    lengths = draw_lengths(jax.random.fold_in(seeds[4], 71), 0)
    return dict(video_clips=video_clips, cotangent=cotangent, weight=weight, lengths=lengths)


def swish_grad(values):
    sig = jax.nn.sigmoid(values)
    return sig * (1.0 + values * (1.0 - sig))

def reference(video_clips, cotangent, weight, lengths):
    positions = jnp.arange(FRAMES, dtype=jnp.int32)
    valid = (positions[None, :] < lengths[:, None]).astype(jnp.float32)[:, :, None, None, None]
    inputs = video_clips.astype(jnp.float32)
    activated = (jax.nn.silu(inputs) * valid).astype(jnp.bfloat16)
    grad_out = (cotangent.astype(jnp.float32) * valid).astype(jnp.bfloat16)
    rows = CLIPS * FRAMES * HEIGHT * WIDTH
    padded_act = jnp.pad(activated, ((0, 0), (2, 0), (1, 1), (1, 1), (0, 0)))
    padded_grad = jnp.pad(grad_out, ((0, 0), (0, 2), (1, 1), (1, 1), (0, 0)))
    grad_rows = grad_out.reshape(rows, CHANNELS)
    forward_sum = jnp.zeros((rows, CHANNELS), jnp.float32)
    back_sum = jnp.zeros((rows, CHANNELS), jnp.float32)
    kernel_terms = []
    for tap_time in range(3):
        for tap_row in range(3):
            for tap_col in range(3):
                window = padded_act[:, tap_time:tap_time + FRAMES, tap_row:tap_row + HEIGHT, tap_col:tap_col + WIDTH].reshape(rows, CHANNELS)
                forward_sum = forward_sum + jnp.dot(window, weight[tap_time, tap_row, tap_col], preferred_element_type=jnp.float32)
                kernel_terms.append(lax.dot_general(window, grad_rows, (((0,), (0,)), ((), ())), preferred_element_type=jnp.float32))
                sliced = padded_grad[:, 2 - tap_time:2 - tap_time + FRAMES, 2 - tap_row:2 - tap_row + HEIGHT, 2 - tap_col:2 - tap_col + WIDTH].reshape(rows, CHANNELS)
                back_sum = back_sum + lax.dot_general(sliced, weight[tap_time, tap_row, tap_col], (((1,), (1,)), ((), ())), preferred_element_type=jnp.float32)
    shape = (CLIPS, FRAMES, HEIGHT, WIDTH, CHANNELS)
    conv_out = (forward_sum.reshape(shape) * valid).astype(jnp.bfloat16)
    input_grad = (back_sum.reshape(shape) * swish_grad(inputs) * valid / CLIPS).astype(jnp.bfloat16)
    weight_grad = jnp.stack(kernel_terms).reshape(3, 3, 3, CHANNELS, CHANNELS) / CLIPS
    return (conv_out, input_grad, weight_grad)
```

```python
import functools

import jax
import jax.numpy as jnp
from jax import lax
from jax.experimental import pallas as pl
from jax.experimental.pallas import tpu as pltpu
from jax.sharding import PartitionSpec as P

F32 = jnp.float32
BF16 = jnp.bfloat16
LANES = 128
VMEM = pl.BlockSpec(memory_space=pltpu.VMEM)
SMEM = pl.BlockSpec(memory_space=pltpu.SMEM)


def call(body, outs, args, *, specs=None, scratch=(), flops=0, name=None):
    moved = sum(a.size * a.dtype.itemsize for a in (*args, *outs))
    return pl.pallas_call(
        body,
        out_shape=tuple(jax.ShapeDtypeStruct(o.shape, o.dtype) for o in outs),
        in_specs=specs or [VMEM] * len(args),
        out_specs=tuple(VMEM for _ in outs),
        scratch_shapes=list(scratch),
        cost_estimate=pl.CostEstimate(flops=flops, bytes_accessed=moved, transcendentals=0),
        name=name,
    )(*args)


def sds(shape, dtype):
    return jax.ShapeDtypeStruct(shape, dtype)


def swap(value, axis, mask):
    count = lax.axis_size(axis)
    return lax.ppermute(value, axis, [(s, s ^ mask) for s in range(count)])


def low_half(shape):
    return lax.broadcasted_iota(jnp.int32, shape, len(shape) - 1) < LANES // 2


def half_turn(value):
    return pltpu.roll(value, LANES // 2, axis=1)


def column_shift(value, step, width):
    if step == 0:
        return value
    rows = value.shape[0]
    turned = pltpu.roll(value, (-step) % rows, axis=0)
    column = lax.broadcasted_iota(jnp.int32, value.shape, 0) % width
    edge = width - 1 if step > 0 else 0
    return jnp.where(column == edge, jnp.zeros_like(turned), turned)


def row_shift(value, step, width):
    if step == 0:
        return value
    blank = jnp.zeros((width, value.shape[1]), value.dtype)
    if step > 0:
        return jnp.concatenate([value[width:], blank], axis=0)
    return jnp.concatenate([blank, value[:-width]], axis=0)


def valid_frame(length_ref, frame, frame_count):
    first = lax.axis_index("tm") * frame_count
    return jnp.where(first + frame < length_ref[0], 1.0, 0.0).astype(F32)


def prepare_body(peers, area, length_ref, clips_ref, cot_ref, grad_ref, *rest):
    packs, picks = rest[:peers], rest[peers]
    me = lax.axis_index("tm")
    wide = clips_ref.shape[1]
    per_peer = wide // peers
    halves = LANES // per_peer
    masked = []
    for frame in range(2):
        rows = pl.ds(frame * area, area)
        keep = valid_frame(length_ref, frame, 2)
        values = clips_ref[rows, :].astype(F32)
        act = (jax.nn.silu(values) * keep).astype(BF16)
        for pack in packs:
            pack[rows, :] = act
        grad = cot_ref[rows, :].astype(F32) * keep
        grad_ref[rows, :] = grad.astype(BF16)
        masked.append(grad)
    low = low_half((area, LANES))
    for tile in range(wide // LANES):
        lanes = slice(tile * LANES, (tile + 1) * LANES)
        first, second = masked[0][:, lanes], masked[1][:, lanes]
        picks[tile * halves] = jnp.where(low, first, half_turn(second))
        picks[tile * halves + 1] = jnp.where(low, half_turn(first), second)
    for mask, pack in enumerate(packs):
        mine = picks[me ^ mask].astype(BF16)
        pack[2 * area :, :LANES] = mine[: area // 2]
        pack[2 * area :, LANES:] = mine[area // 2 :]


def kernel_grad_body(peers, area, width, parts, *refs):
    packs = refs[:peers]
    keep_ref, send_ref, act_t, grads = refs[peers:]
    me = lax.axis_index("tm")
    core = lax.axis_index("dp") % 2
    block = 2 * area
    low = low_half((area, LANES))
    for mask, pack in enumerate(packs):
        start = pl.multiple_of((me ^ mask) * block, block)
        for frame in range(2):
            act = pack[frame * area : (frame + 1) * area, :]
            act_t[:, pl.ds(start + frame * area, area)] = act.T
        both = jnp.concatenate([pack[block:, :LANES], pack[block:, LANES:]], axis=0).astype(F32)
        taps = []
        for row_tap in range(3):
            for col_tap in range(3):
                moved = column_shift(both, 1 - col_tap, width)
                turned = half_turn(moved)
                taps.append([row_shift(v, 1 - row_tap, width) for v in (moved, turned)])
        blank = [jnp.zeros_like(both)] * 2
        taps.append(blank)
        for tile in range(5):
            (even, even_turned), (odd, odd_turned) = taps[2 * tile], taps[2 * tile + 1]
            for frame in range(2):
                left, right = (even, odd_turned) if frame == 0 else (even_turned, odd)
                grads[pl.ds(start + frame * area, area), tile * LANES : (tile + 1) * LANES] = (
                    jnp.where(low, left, right).astype(BF16)
                )
    frames = 2 * peers
    sums = []
    for time_tap in range(3):
        used = (frames - 2 + time_tap) * area
        sums.append(
            jnp.dot(
                act_t[:, :used],
                grads[(2 - time_tap) * area :, :],
                preferred_element_type=F32,
            )
        )
    tiles = [s[:, tile * LANES : (tile + 1) * LANES] for s in sums for tile in range(4)]
    last = [s[:, 4 * LANES :] for s in sums]
    top = low_half(last[0].shape)
    tiles.append(jnp.where(top, last[0], half_turn(last[1])))
    tiles.append(last[2])
    count = keep_ref.shape[1]
    groups = [
        [t[(2 * z + c) * count : (2 * z + c + 1) * count] for t in tiles]
        for z in range(parts)
        for c in range(2)
    ]
    for own in range(2):

        @pl.when(core == own)
        def _(own=own):
            for z in range(parts):
                for at in range(len(tiles)):
                    lanes = slice(at * LANES, (at + 1) * LANES)
                    keep_ref[z, :, lanes] = groups[2 * z + own][at]
                    send_ref[z, :, lanes] = groups[2 * z + 1 - own][at].astype(BF16)


def sum_body(arrived, radix, step, *refs):
    keep_ref, in_refs = refs[0], refs[1 : 1 + arrived]
    total = keep_ref[...]
    for ref in in_refs:
        total = total + ref[...].astype(F32)
    if radix == 1:
        refs[1 + arrived][...] = total[0].astype(BF16)
        return
    out_refs, held = refs[1 + arrived : -1], refs[-1]
    held[...] = total
    digit = (lax.axis_index("dp") // 2) // step % radix
    for mask, out in enumerate(out_refs):
        out[...] = held[pl.ds((digit ^ mask) * step, step)].astype(out.dtype)


def sum_over_clips(keep, send):
    arrived = [swap(send, "dp", 1)]
    while True:
        parts, count, lanes = keep.shape
        radix = 1 if parts == 1 else (4 if parts % 4 == 0 else 2)
        assert parts % radix == 0 and radix & (radix - 1) == 0, "dp size"
        step = parts // radix
        if radix == 1:
            return call(
                functools.partial(sum_body, len(arrived), 1, 1),
                [sds((count, lanes), BF16)],
                (keep, *arrived),
                name="sum_last",
            )[0]
        outs = [sds((step, count, lanes), F32)]
        outs += [sds((step, count, lanes), BF16)] * (radix - 1)
        keep, *sends = call(
            functools.partial(sum_body, len(arrived), radix, step),
            outs,
            (keep, *arrived),
            scratch=[pltpu.VMEM((parts, count, lanes), F32)],
            name="sum_cut",
        )
        arrived = [swap(s, "dp", 2 * step * (m + 1)) for m, s in enumerate(sends)]


def place_body(peers, scale, *refs):
    pieces, out_ref, held = refs[:peers], refs[peers], refs[peers + 1]
    me = lax.axis_index("tm")
    for mask, piece in enumerate(pieces):
        held[me ^ mask] = piece[...].astype(F32) * scale
    low = low_half((held.shape[1], LANES))
    for time_tap in range(3):
        for tap in range(9):
            tile = 4 * time_tap + tap // 2 if tap < 8 else 12 + time_tap // 2
            half = tap % 2 if tap < 8 else time_tap % 2
            for pair in range(peers // 2):
                left = held[2 * pair, :, tile * LANES : (tile + 1) * LANES]
                right = held[2 * pair + 1, :, tile * LANES : (tile + 1) * LANES]
                if half == 0:
                    value = jnp.where(low, left, half_turn(right))
                else:
                    value = jnp.where(low, half_turn(left), right)
                out_ref[9 * time_tap + tap, :, pair * LANES : (pair + 1) * LANES] = value


def fill_padded(out_ref, frame, value, width, height, direction):
    wide = value.shape[1]
    blank = jnp.zeros((width, 3 * wide), BF16)
    out_ref[frame, :width, :] = blank
    out_ref[frame, (height + 1) * width :, :] = blank
    for tap in range(3):
        out_ref[frame, width : (height + 1) * width, tap * wide : (tap + 1) * wide] = column_shift(
            value, direction * (tap - 1), width
        ).astype(BF16)


def conv_body(peers, area, width, total_clips, length_ref, *refs):
    packs = refs[:peers]
    grad_ref, later_ref, clips_ref, w_ref, wt_ref, out_ref, gin_ref, acts, grads = refs[peers:]
    me = lax.axis_index("tm")
    height = area // width
    for frame in range(2):
        rows = slice(frame * area, (frame + 1) * area)
        value = jnp.zeros((area, acts.shape[2] // 3), F32)
        for mask in range(1, peers):
            if mask & (mask + 1) == 0:
                value = jnp.where((me ^ mask) == me - 1, packs[mask][rows, :].astype(F32), value)
        fill_padded(acts, frame, value, width, height, 1)
        fill_padded(acts, 2 + frame, packs[0][rows, :].astype(F32), width, height, 1)
        fill_padded(grads, frame, grad_ref[rows, :].astype(F32), width, height, -1)
        fill_padded(grads, 2 + frame, later_ref[rows, :].astype(F32), width, height, -1)
    for frame in range(2):
        rows = slice(frame * area, (frame + 1) * area)
        keep = valid_frame(length_ref, frame, 2)
        total = jnp.zeros((area, out_ref.shape[1]), F32)
        for time_tap in range(3):
            for row_tap in range(3):
                window = acts[frame + time_tap, row_tap * width : row_tap * width + area, :]
                total = total + jnp.dot(
                    window, w_ref[3 * time_tap + row_tap], preferred_element_type=F32
                )
        out_ref[rows, :] = (total * keep).astype(BF16)
        total = jnp.zeros((area, out_ref.shape[1]), F32)
        for time_tap in range(3):
            for row_tap in range(3):
                first = (2 - row_tap) * width
                window = grads[frame + 2 - time_tap, first : first + area, :]
                total = total + jnp.dot(
                    window, wt_ref[3 * time_tap + row_tap], preferred_element_type=F32
                )
        values = clips_ref[rows, :].astype(F32)
        sig = jax.nn.sigmoid(values)
        slope = sig * (1.0 + values * (1.0 - sig))
        gin_ref[rows, :] = (total * slope * (keep / total_clips)).astype(BF16)


def turn_body(w_ref, out_ref):
    wide = w_ref.shape[2]
    for tap in range(w_ref.shape[0]):
        at = tap % 3 * wide
        out_ref[tap // 3, at : at + wide, :] = w_ref[tap].T


def local(video_clips, cotangent, weight, lengths):
    clip_count, frame_count, height, width, channels = video_clips.shape
    peers, shards = lax.axis_size("tm"), lax.axis_size("dp")
    total_clips = clip_count * shards
    area = height * width
    assert clip_count == 1 and frame_count == 2, "block shape"
    assert 2 * channels == peers * LANES and peers & (peers - 1) == 0, "tm size"
    clips = video_clips.reshape(2 * area, channels)
    cot = cotangent.reshape(2 * area, channels)

    block = (2 * area, channels)
    pack = sds((2 * area + area // 2, channels), BF16)
    grad, *packs = call(
        functools.partial(prepare_body, peers, area),
        [sds(block, BF16)] + [pack] * peers,
        (lengths, clips, cot),
        specs=[SMEM, VMEM, VMEM],
        scratch=[pltpu.VMEM((peers, area, LANES), F32)],
        name="prepare",
    )
    got = [packs[0]] + [swap(packs[m], "tm", m) for m in range(1, peers)]
    later = lax.ppermute(grad, "tm", [(s, s - 1) for s in range(1, peers)])

    flat = weight.reshape(9, 3 * channels, channels)
    (turned,) = call(
        turn_body, [flat], (weight.reshape(27, channels, channels),), name="turn_weight"
    )

    parts = shards // 2
    count = channels // shards
    lanes = 14 * LANES
    keep, send = call(
        functools.partial(kernel_grad_body, peers, area, width, parts),
        [sds((parts, count, lanes), F32), sds((parts, count, lanes), BF16)],
        got,
        scratch=[
            pltpu.VMEM((channels, 2 * peers * area), BF16),
            pltpu.VMEM((2 * peers * area, 5 * LANES), BF16),
        ],
        flops=2 * 27 * 2 * peers * area * channels * LANES // 2,
        name="kernel_grad",
    )
    conv_out, input_grad = call(
        functools.partial(conv_body, peers, area, width, total_clips),
        [sds(block, BF16)] * 2,
        (lengths, *got, grad, later, clips, flat, turned),
        specs=[SMEM] + [VMEM] * (peers + 5),
        scratch=[pltpu.VMEM((4, area + 2 * width, 3 * channels), BF16)] * 2,
        flops=2 * 2 * 27 * 2 * area * channels * channels,
        name="conv",
    )
    piece = sum_over_clips(keep, send)
    pieces = [piece] + [swap(piece, "tm", m) for m in range(1, peers)]
    (placed,) = call(
        functools.partial(place_body, peers, 1.0 / total_clips),
        [sds((27, count, channels), F32)],
        pieces,
        scratch=[pltpu.VMEM((peers, count, lanes), F32)],
        name="place",
    )
    shape = video_clips.shape
    weight_grad = placed.reshape(3, 3, 3, count, channels)
    return conv_out.reshape(shape), input_grad.reshape(shape), weight_grad


def solution(mesh):
    in_specs = (P("dp", "tm", None, None, None), P("dp", "tm", None, None, None), P(), P("dp"))
    out_specs = (
        P("dp", "tm", None, None, None),
        P("dp", "tm", None, None, None),
        P(None, None, None, "dp", None),
    )
    return jax.shard_map(local, mesh=mesh, in_specs=in_specs, out_specs=out_specs, check_vma=False)
```

```python
import functools

import jax
import jax.numpy as jnp
from jax import lax
from jax.experimental import pallas as pl
from jax.experimental.pallas import tpu as pltpu
from jax.sharding import PartitionSpec as P


F32 = jnp.float32
BF16 = jnp.bfloat16
LANES = 128
VMEM = pl.BlockSpec(memory_space=pltpu.VMEM)


def call(body, outs, args, *, after=(), resident=True, scratch=(), flops=0):
    moved = sum(a.size * a.dtype.itemsize for a in args)
    space = pltpu.VMEM if resident else pltpu.HBM
    held = [a if a.size == 1 else pltpu.with_memory_space_constraint(a, space) for a in args]
    count = len(args)

    def with_after(*refs):
        body(*refs[:count], *refs[count + len(after) :])

    return pl.pallas_call(
        with_after,
        out_shape=tuple(outs),
        in_specs=[pl.BlockSpec(memory_space=pltpu.SMEM if a.size == 1 else space) for a in args]
        + [pl.BlockSpec(memory_space=pl.ANY)] * len(after),
        out_specs=tuple(VMEM for _ in outs),
        scratch_shapes=list(scratch),
        compiler_params=pltpu.CompilerParams(vmem_limit_bytes=32 << 20),
        cost_estimate=pl.CostEstimate(flops=flops, bytes_accessed=moved, transcendentals=0),
    )(*held, *after)


def sds(shape, dtype):
    return jax.ShapeDtypeStruct(shape, dtype)


def swap(value, axis, mask):
    count = lax.axis_size(axis)
    return lax.ppermute(value, axis, [(s, s ^ mask) for s in range(count)])


def low_half(shape):
    return lax.broadcasted_iota(jnp.int32, shape, len(shape) - 1) < LANES // 2


def half_turn(value):
    return pltpu.roll(value, LANES // 2, axis=1)


def column_shift(value, step, width):
    if step == 0:
        return value
    rows = value.shape[0]
    turned = pltpu.roll(value, (-step) % rows, axis=0)
    column = lax.broadcasted_iota(jnp.int32, value.shape, 0) % width
    edge = width - 1 if step > 0 else 0
    return jnp.where(column == edge, jnp.zeros_like(turned), turned)


def row_shift(value, step, width):
    if step == 0:
        return value
    blank = jnp.zeros((width, value.shape[1]), value.dtype)
    if step > 0:
        return jnp.concatenate([value[width:], blank], axis=0)
    return jnp.concatenate([blank, value[:-width]], axis=0)


def prepare_body(peers, area, length_ref, clips_hbm, cot_hbm, grad_ref, keep_ref, *rest):
    packs = rest[:peers]
    clips, cot, picks, sems = rest[peers:]
    me = lax.axis_index("tm")
    wide = clips.shape[1]
    per_peer = wide // peers
    halves = LANES // per_peer
    copies = []
    for frame in range(2):
        rows = pl.ds(frame * area, area)
        for at, (source, held) in enumerate(((cot_hbm, cot), (clips_hbm, clips))):
            copies.append(
                pltpu.make_async_copy(
                    source.at[rows, :], held.at[rows, :], sems.at[2 * frame + at]
                )
            )
    for copy in copies:
        copy.start()
    masked = []
    for frame in range(2):
        rows = pl.ds(frame * area, area)
        keep = jnp.where(me * 2 + frame < length_ref[0], 1.0, 0.0).astype(F32)
        keep_ref[frame : frame + 1, :] = jnp.full((1, wide), keep, F32)
        copies[2 * frame].wait()
        grad = cot[rows, :].astype(F32) * keep
        grad_ref[rows, :] = grad.astype(BF16)
        masked.append(grad)
        copies[2 * frame + 1].wait()
        values = clips[rows, :].astype(F32)
        act = (jax.nn.silu(values) * keep).astype(BF16)
        for pack in packs:
            pack[rows, :] = act
    low = low_half((area, LANES))
    for tile in range(wide // LANES):
        lanes = slice(tile * LANES, (tile + 1) * LANES)
        first, second = masked[0][:, lanes], masked[1][:, lanes]
        picks[tile * halves] = jnp.where(low, first, half_turn(second))
        picks[tile * halves + 1] = jnp.where(low, half_turn(first), second)
    for mask, pack in enumerate(packs):
        mine = picks[me ^ mask].astype(BF16)
        pack[2 * area :, :LANES] = mine[: area // 2]
        pack[2 * area :, LANES:] = mine[area // 2 :]


def kernel_grad_body(peers, area, width, parts, *refs):
    packs = refs[:peers]
    keep_ref, send_ref, act_t, grads = refs[peers:]
    me = lax.axis_index("tm")
    core = lax.axis_index("dp") % 2
    block = 2 * area
    low = low_half((area, LANES))
    for mask, pack in enumerate(packs):
        start = pl.multiple_of((me ^ mask) * block, block)
        for frame in range(2):
            act = pack[frame * area : (frame + 1) * area, :]
            act_t[:, pl.ds(start + frame * area, area)] = act.T
        both = jnp.concatenate([pack[block:, :LANES], pack[block:, LANES:]], axis=0).astype(F32)
        taps = []
        for row_tap in range(3):
            for col_tap in range(3):
                moved = column_shift(both, 1 - col_tap, width)
                turned = half_turn(moved)
                taps.append([row_shift(v, 1 - row_tap, width) for v in (moved, turned)])
        blank = [jnp.zeros_like(both)] * 2
        taps.append(blank)
        for tile in range(5):
            (even, even_turned), (odd, odd_turned) = taps[2 * tile], taps[2 * tile + 1]
            for frame in range(2):
                left, right = (even, odd_turned) if frame == 0 else (even_turned, odd)
                grads[pl.ds(start + frame * area, area), tile * LANES : (tile + 1) * LANES] = (
                    jnp.where(low, left, right).astype(BF16)
                )
    frames = 2 * peers
    sums = []
    for time_tap in range(3):
        used = (frames - 2 + time_tap) * area
        sums.append(
            jnp.dot(
                act_t[:, :used],
                grads[(2 - time_tap) * area :, :],
                preferred_element_type=F32,
            )
        )
    tiles = [s[:, tile * LANES : (tile + 1) * LANES] for s in sums for tile in range(4)]
    last = [s[:, 4 * LANES :] for s in sums]
    top = low_half(last[0].shape)
    tiles.append(jnp.where(top, last[0], half_turn(last[1])))
    tiles.append(last[2])
    count = keep_ref.shape[1]
    groups = [
        [t[(2 * z + c) * count : (2 * z + c + 1) * count] for t in tiles]
        for z in range(parts)
        for c in range(2)
    ]
    for own in range(2):

        @pl.when(core == own)
        def _(own=own):
            for z in range(parts):
                for at in range(len(tiles)):
                    lanes = slice(at * LANES, (at + 1) * LANES)
                    keep_ref[z, :, lanes] = groups[2 * z + own][at]
                    send_ref[z, :, lanes] = groups[2 * z + 1 - own][at].astype(BF16)


def sum_body(arrived, radix, step, *refs):
    keep_ref, in_refs = refs[0], refs[1 : 1 + arrived]
    total = keep_ref[...]
    for ref in in_refs:
        total = total + ref[...].astype(F32)
    if radix == 1:
        refs[1 + arrived][...] = total[0].astype(BF16)
        return
    out_refs, held = refs[1 + arrived : -1], refs[-1]
    held[...] = total
    digit = (lax.axis_index("dp") // 2) // step % radix
    for mask, out in enumerate(out_refs):
        out[...] = held[pl.ds((digit ^ mask) * step, step)].astype(out.dtype)


def sum_over_clips(keep, send, after):
    arrived = [swap(send, "dp", 1)]
    while True:
        parts, count, lanes = keep.shape
        radix = 1 if parts == 1 else (4 if parts % 4 == 0 else 2)
        assert parts % radix == 0 and radix & (radix - 1) == 0, "dp size"
        step = parts // radix
        if radix == 1:
            return call(
                functools.partial(sum_body, len(arrived), 1, 1),
                [pltpu.VMEM((count, lanes), BF16)],
                (keep, *arrived),
                after=after,
            )[0]
        outs = [pltpu.VMEM((step, count, lanes), F32)]
        outs += [pltpu.VMEM((step, count, lanes), BF16)] * (radix - 1)
        keep, *sends = call(
            functools.partial(sum_body, len(arrived), radix, step),
            outs,
            (keep, *arrived),
            scratch=[pltpu.VMEM((parts, count, lanes), F32)],
        )
        arrived = [swap(s, "dp", 2 * step * (m + 1)) for m, s in enumerate(sends)]


def place_body(peers, scale, *refs):
    pieces, out_ref, held = refs[:peers], refs[peers], refs[peers + 1]
    me = lax.axis_index("tm")
    for mask, piece in enumerate(pieces):
        held[me ^ mask] = piece[...].astype(F32) * scale
    low = low_half((held.shape[1], LANES))
    for time_tap in range(3):
        for tap in range(9):
            tile = 4 * time_tap + tap // 2 if tap < 8 else 12 + time_tap // 2
            half = tap % 2 if tap < 8 else time_tap % 2
            for pair in range(peers // 2):
                left = held[2 * pair, :, tile * LANES : (tile + 1) * LANES]
                right = held[2 * pair + 1, :, tile * LANES : (tile + 1) * LANES]
                if half == 0:
                    value = jnp.where(low, left, half_turn(right))
                else:
                    value = jnp.where(low, half_turn(left), right)
                out_ref[9 * time_tap + tap, :, pair * LANES : (pair + 1) * LANES] = value


def fill_padded(out_ref, frame, value, width, height, direction):
    wide = value.shape[1]
    blank = jnp.zeros((width, 3 * wide), BF16)
    out_ref[frame, :width, :] = blank
    out_ref[frame, (height + 1) * width :, :] = blank
    for tap in range(3):
        out_ref[frame, width : (height + 1) * width, tap * wide : (tap + 1) * wide] = column_shift(
            value, direction * (tap - 1), width
        ).astype(BF16)


def conv_body(peers, area, width, total_clips, keep_ref, *refs):
    packs = refs[:peers]
    grad_ref, later_ref, clips_ref, w_ref, wt_ref = refs[peers : peers + 5]
    out_ref, gin_ref, token_ref, acts, grads = refs[peers + 5 :]
    token_ref[...] = jnp.zeros_like(token_ref)
    me = lax.axis_index("tm")
    height = area // width
    for frame in range(2):
        rows = slice(frame * area, (frame + 1) * area)
        value = jnp.zeros((area, acts.shape[2] // 3), F32)
        for mask in range(1, peers):
            if mask & (mask + 1) == 0:
                value = jnp.where((me ^ mask) == me - 1, packs[mask][rows, :].astype(F32), value)
        fill_padded(acts, frame, value, width, height, 1)
        fill_padded(acts, 2 + frame, packs[0][rows, :].astype(F32), width, height, 1)
        fill_padded(grads, frame, grad_ref[rows, :].astype(F32), width, height, -1)
        fill_padded(grads, 2 + frame, later_ref[rows, :].astype(F32), width, height, -1)
    for frame in range(2):
        rows = slice(frame * area, (frame + 1) * area)
        keep = keep_ref[frame : frame + 1, :]
        total = jnp.zeros((area, out_ref.shape[1]), F32)
        for time_tap in range(3):
            for row_tap in range(3):
                window = acts[frame + time_tap, row_tap * width : row_tap * width + area, :]
                total = total + jnp.dot(
                    window, w_ref[3 * time_tap + row_tap], preferred_element_type=F32
                )
        out_ref[rows, :] = (total * keep).astype(BF16)
        total = jnp.zeros((area, out_ref.shape[1]), F32)
        for time_tap in range(3):
            for row_tap in range(3):
                first = (2 - row_tap) * width
                window = grads[frame + 2 - time_tap, first : first + area, :]
                total = total + jnp.dot(
                    window, wt_ref[3 * time_tap + row_tap], preferred_element_type=F32
                )
        values = clips_ref[rows, :].astype(F32)
        sig = jax.nn.sigmoid(values)
        slope = sig * (1.0 + values * (1.0 - sig))
        gin_ref[rows, :] = (total * slope * (keep / total_clips)).astype(BF16)


def turn_body(w_ref, out_ref):
    wide = w_ref.shape[2]
    for tap in range(w_ref.shape[0]):
        at = tap % 3 * wide
        out_ref[tap // 3, at : at + wide, :] = w_ref[tap].T


def local(video_clips, cotangent, weight, lengths):
    clip_count, frame_count, height, width, channels = video_clips.shape
    peers, shards = lax.axis_size("tm"), lax.axis_size("dp")
    total_clips = clip_count * shards
    area = height * width
    assert clip_count == 1 and frame_count == 2, "block shape"
    assert 2 * channels == peers * LANES and peers & (peers - 1) == 0, "tm size"
    clips = video_clips.reshape(2 * area, channels)
    cot = cotangent.reshape(2 * area, channels)

    block = (2 * area, channels)
    pack = pltpu.VMEM((2 * area + area // 2, channels), BF16)
    grad, keep, *packs = call(
        functools.partial(prepare_body, peers, area),
        [pltpu.VMEM(block, BF16), pltpu.VMEM((8, channels), F32)] + [pack] * peers,
        (lengths, clips, cot),
        resident=False,
        scratch=[
            pltpu.VMEM(block, BF16),
            pltpu.VMEM(block, BF16),
            pltpu.VMEM((peers, area, LANES), F32),
            pltpu.SemaphoreType.DMA((4,)),
        ],
    )
    got = [packs[0]] + [swap(packs[m], "tm", m) for m in range(1, peers)]
    later = lax.ppermute(grad, "tm", [(s, s - 1) for s in range(1, peers)])

    flat = weight.reshape(9, 3 * channels, channels)
    (turned,) = call(
        turn_body, [pltpu.VMEM(flat.shape, BF16)], (weight.reshape(27, channels, channels),)
    )

    parts = shards // 2
    count = channels // shards
    lanes = 14 * LANES
    mine, send = call(
        functools.partial(kernel_grad_body, peers, area, width, parts),
        [pltpu.VMEM((parts, count, lanes), F32), pltpu.VMEM((parts, count, lanes), BF16)],
        got,
        after=(turned,),
        scratch=[
            pltpu.VMEM((channels, 2 * peers * area), BF16),
            pltpu.VMEM((2 * peers * area, 5 * LANES), BF16),
        ],
        flops=2 * 27 * 2 * peers * area * channels * LANES // 2,
    )
    conv_out, input_grad, token = call(
        functools.partial(conv_body, peers, area, width, total_clips),
        [sds(block, BF16)] * 2 + [pltpu.VMEM((8, LANES), F32)],
        (keep, *got, grad, later, clips, flat, turned),
        scratch=[pltpu.VMEM((4, area + 2 * width, 3 * channels), BF16)] * 2,
        flops=2 * 2 * 27 * 2 * area * channels * channels,
    )
    piece = sum_over_clips(mine, send, (token,))
    pieces = [piece] + [swap(piece, "tm", m) for m in range(1, peers)]
    (placed,) = call(
        functools.partial(place_body, peers, 1.0 / total_clips),
        [sds((27, count, channels), F32)],
        pieces,
        scratch=[pltpu.VMEM((peers, count, lanes), F32)],
    )
    shape = video_clips.shape
    weight_grad = placed.reshape(3, 3, 3, count, channels)
    return conv_out.reshape(shape), input_grad.reshape(shape), weight_grad


def solution(mesh):
    in_specs = (P("dp", "tm", None, None, None), P("dp", "tm", None, None, None), P(), P("dp"))
    out_specs = (
        P("dp", "tm", None, None, None),
        P("dp", "tm", None, None, None),
        P(None, None, None, "dp", None),
    )

    return jax.shard_map(local, mesh=mesh, in_specs=in_specs, out_specs=out_specs, check_vma=False)
```

```python
import functools

import jax
import jax.numpy as jnp
from jax import lax
from jax.experimental import pallas as pl
from jax.experimental.pallas import tpu as pltpu
from jax.sharding import PartitionSpec as P


F32 = jnp.float32
BF16 = jnp.bfloat16
LANES = 128
VMEM = pl.BlockSpec(memory_space=pltpu.VMEM)


def call(body, outs, args, *, after=(), resident=True, scratch=(), flops=0, aliases=None):
    moved = sum(a.size * a.dtype.itemsize for a in args)
    space = pltpu.VMEM if resident else pltpu.HBM
    held = [a if a.size == 1 else pltpu.with_memory_space_constraint(a, space) for a in args]
    count = len(args)

    def with_after(*refs):
        body(*refs[:count], *refs[count + len(after) :])

    return pl.pallas_call(
        with_after,
        out_shape=tuple(outs),
        in_specs=[pl.BlockSpec(memory_space=pltpu.SMEM if a.size == 1 else space) for a in args]
        + [pl.BlockSpec(memory_space=pl.ANY)] * len(after),
        out_specs=tuple(VMEM for _ in outs),
        scratch_shapes=list(scratch),
        input_output_aliases=aliases or {},
        compiler_params=pltpu.CompilerParams(vmem_limit_bytes=32 << 20),
        cost_estimate=pl.CostEstimate(flops=flops, bytes_accessed=moved, transcendentals=0),
    )(*held, *after)


def sds(shape, dtype):
    return jax.ShapeDtypeStruct(shape, dtype)


def swap(value, axis, mask):
    count = lax.axis_size(axis)
    return lax.ppermute(value, axis, [(s, s ^ mask) for s in range(count)])


def swaps(values, axis, step):
    got = []
    for m, value in enumerate(values):
        got.append(swap(value, axis, (m + 1) * step))
    return got


def low_half(shape):
    return lax.broadcasted_iota(jnp.int32, shape, len(shape) - 1) < LANES // 2


def half_turn(value):
    return pltpu.roll(value, LANES // 2, axis=1)


def column_shift(value, step, width):
    if step == 0:
        return value
    rows = value.shape[0]
    turned = pltpu.roll(value, (-step) % rows, axis=0)
    column = lax.broadcasted_iota(jnp.int32, value.shape, 0) % width
    edge = width - 1 if step > 0 else 0
    return jnp.where(column == edge, jnp.zeros_like(turned), turned)


def row_shift(value, step, width):
    if step == 0:
        return value
    blank = jnp.zeros((width, value.shape[1]), value.dtype)
    if step > 0:
        return jnp.concatenate([value[width:], blank], axis=0)
    return jnp.concatenate([blank, value[:-width]], axis=0)


def kept(length_ref, frame):
    return jnp.where(frame < length_ref[0], 1.0, 0.0).astype(F32)


def slice_body(peers, area, cot_hbm, clips_hbm, *refs):
    outs, own = refs[:peers], refs[peers]
    cot, picks, sems = refs[peers + 1 :]
    me = lax.axis_index("tm")
    copies = []
    for tile in range(cot.shape[0]):
        lanes = pl.ds(tile * LANES, LANES)
        copies.append(pltpu.make_async_copy(cot_hbm.at[:, lanes], cot.at[tile], sems.at[tile]))
    own_copy = pltpu.make_async_copy(clips_hbm, own, sems.at[len(copies)])
    for copy in (*copies, own_copy):
        copy.start()
    low = low_half((area, LANES))
    halves = peers // len(copies)
    for tile, copy in enumerate(copies):
        copy.wait()
        first = cot[tile, :area, :].astype(F32)
        second = cot[tile, area:, :].astype(F32)
        picks[tile * halves] = jnp.where(low, first, half_turn(second))
        picks[tile * halves + 1] = jnp.where(low, half_turn(first), second)
    for mask, out in enumerate(outs):
        out[...] = picks[me ^ mask].astype(BF16)
    own_copy.wait()


def place_grads_body(peers, area, width, length_ref, *refs):
    slices, grads = refs[:peers], refs[peers]
    me = lax.axis_index("tm")
    grads[2 * peers * area :, :] = jnp.zeros((2 * area, grads.shape[1]), BF16)
    low = low_half((area, LANES))
    for mask, ref in enumerate(slices):
        start = pl.multiple_of((me ^ mask) * 2 * area, 2 * area)
        first = 2 * (me ^ mask)
        keep = jnp.where(low, kept(length_ref, first), kept(length_ref, first + 1))
        both = ref[...].astype(F32) * keep
        taps = []
        for row_tap in range(3):
            for col_tap in range(3):
                moved = column_shift(both, 1 - col_tap, width)
                turned = half_turn(moved)
                taps.append([row_shift(v, 1 - row_tap, width) for v in (moved, turned)])
        taps.append([jnp.zeros_like(both)] * 2)
        for tile in range(5):
            (even, even_turned), (odd, odd_turned) = taps[2 * tile], taps[2 * tile + 1]
            for frame in range(2):
                left, right = (even, odd_turned) if frame == 0 else (even_turned, odd)
                grads[pl.ds(start + frame * area, area), tile * LANES : (tile + 1) * LANES] = (
                    jnp.where(low, left, right).astype(BF16)
                )


def cut_body(start, source, out_ref):
    out_ref[...] = source[start : start + out_ref.shape[0], :]


def turn_frame(act_t, block, frame, values):
    area = values.shape[0]
    at = pl.multiple_of((2 * block + frame) * area, area)
    act_t[:, pl.ds(at, area)] = jax.nn.silu(values.astype(F32)).astype(BF16).T


def turn_blocks_body(area, *refs):
    act_t = refs[-1]
    me = lax.axis_index("tm")
    for mask, ref in enumerate(refs[:-1]):
        for frame in range(2):
            turn_frame(act_t, me ^ mask, frame, ref[frame * area : (frame + 1) * area, :])
    at = pl.multiple_of(2 * (me ^ 3) * area, area)
    act_t[:, pl.ds(at, 2 * area)] = jnp.zeros((act_t.shape[0], 2 * area), BF16)


def products_body(peers, area, grads, act_t, *outs):
    for time_tap, out in enumerate(outs):
        used = (2 * peers - 2 + time_tap) * area
        first = (2 - time_tap) * area
        out[...] = jnp.dot(
            act_t[:, :used], grads[first : first + used, :], preferred_element_type=F32
        )


def kernel_grad_body(area, grads, first, second, *refs):
    held, (keep_ref, send_ref) = refs[:3], refs[3:]
    me = lax.axis_index("tm")
    core = lax.axis_index("dp") % 2
    values = jnp.concatenate([first[...], second[...]], axis=0).astype(F32)
    turned = jax.nn.silu(values).astype(BF16).T
    sums = []
    for time_tap, ref in enumerate(held):
        at = pl.multiple_of((2 * (me ^ 3) + 2 - time_tap) * area, area)
        sums.append(
            ref[...]
            + jnp.dot(turned, grads[pl.ds(at, 2 * area), :], preferred_element_type=F32)
        )
    tiles = [s[:, tile * LANES : (tile + 1) * LANES] for s in sums for tile in range(4)]
    last = [s[:, 4 * LANES :] for s in sums]
    low = low_half(last[0].shape)
    tiles.append(jnp.where(low, last[0], half_turn(last[1])))
    tiles.append(last[2])
    parts, count = keep_ref.shape[:2]
    groups = [
        [t[(2 * z + c) * count : (2 * z + c + 1) * count] for t in tiles]
        for z in range(parts)
        for c in range(2)
    ]
    for own in range(2):

        @pl.when(core == own)
        def _(own=own):
            for z in range(parts):
                for at in range(len(tiles)):
                    lanes = slice(at * LANES, (at + 1) * LANES)
                    keep_ref[z, :, lanes] = groups[2 * z + own][at]
                    send_ref[z, :, lanes] = groups[2 * z + 1 - own][at].astype(BF16)


def sum_body(arrived, radix, step, *refs):
    keep_ref, in_refs = refs[0], refs[1 : 1 + arrived]
    total = keep_ref[...]
    for ref in in_refs:
        total = total + ref[...].astype(F32)
    if radix == 1:
        refs[1 + arrived][...] = total[0].astype(BF16)
        return
    out_refs, held = refs[1 + arrived : -1], refs[-1]
    held[...] = total
    digit = (lax.axis_index("dp") // 2) // step % radix
    for mask, out in enumerate(out_refs):
        out[...] = held[pl.ds((digit ^ mask) * step, step)].astype(out.dtype)


def sum_over_clips(keep, send, after):
    arrived = [swap(send, "dp", 1)]
    while True:
        parts, count, lanes = keep.shape
        radix = 1 if parts == 1 else (4 if parts % 4 == 0 else 2)
        assert parts % radix == 0 and radix & (radix - 1) == 0, "dp size"
        step = parts // radix
        if radix == 1:
            return call(
                functools.partial(sum_body, len(arrived), 1, 1),
                [pltpu.VMEM((count, lanes), BF16)],
                (keep, *arrived),
                after=after,
            )[0]
        outs = [pltpu.VMEM((step, count, lanes), F32)]
        outs += [pltpu.VMEM((step, count, lanes), BF16)] * (radix - 1)
        keep, *sends = call(
            functools.partial(sum_body, len(arrived), radix, step),
            outs,
            (keep, *arrived),
            scratch=[pltpu.VMEM((parts, count, lanes), F32)],
        )
        arrived = swaps(sends, "dp", 2 * step)


def place_body(peers, scale, *refs):
    pieces, out_ref, held = refs[:peers], refs[peers], refs[peers + 1]
    me = lax.axis_index("tm")
    for mask, piece in enumerate(pieces):
        held[me ^ mask] = piece[...].astype(F32) * scale
    low = low_half((held.shape[1], LANES))
    for time_tap in range(3):
        for tap in range(9):
            tile = 4 * time_tap + tap // 2 if tap < 8 else 12 + time_tap // 2
            half = tap % 2 if tap < 8 else time_tap % 2
            for pair in range(peers // 2):
                left = held[2 * pair, :, tile * LANES : (tile + 1) * LANES]
                right = held[2 * pair + 1, :, tile * LANES : (tile + 1) * LANES]
                if half == 0:
                    value = jnp.where(low, left, half_turn(right))
                else:
                    value = jnp.where(low, half_turn(left), right)
                out_ref[9 * time_tap + tap, :, pair * LANES : (pair + 1) * LANES] = value


def fill_padded(out_ref, frame, value, width, height, direction):
    wide = value.shape[1]
    blank = jnp.zeros((width, 3 * wide), BF16)
    out_ref[frame, :width, :] = blank
    out_ref[frame, (height + 1) * width :, :] = blank
    for tap in range(3):
        out_ref[frame, width : (height + 1) * width, tap * wide : (tap + 1) * wide] = column_shift(
            value, direction * (tap - 1), width
        ).astype(BF16)


def ahead_body(area, width, length_ref, own, near, first, second, w_ref, out_ref, token_ref, acts):
    token_ref[...] = jnp.zeros_like(token_ref)
    me = lax.axis_index("tm")
    height = area // width
    far = jnp.concatenate([first[...], second[...]], axis=0)
    for frame in range(2):
        rows = slice(frame * area, (frame + 1) * area)
        value = jnp.where((me ^ 3) == me - 1, far[rows].astype(F32), near[rows, :].astype(F32))
        value = value * jnp.where(me > 0, 1.0, 0.0).astype(F32)
        fill_padded(acts, frame, jax.nn.silu(value), width, height, 1)
        value = own[rows, :].astype(F32)
        fill_padded(acts, 2 + frame, jax.nn.silu(value), width, height, 1)
    for frame in range(2):
        rows = slice(frame * area, (frame + 1) * area)
        total = jnp.zeros((area, out_ref.shape[1]), F32)
        for time_tap in range(3):
            for row_tap in range(3):
                window = acts[frame + time_tap, row_tap * width : row_tap * width + area, :]
                total = total + jnp.dot(
                    window, w_ref[3 * time_tap + row_tap], preferred_element_type=F32
                )
        out_ref[rows, :] = (total * kept(length_ref, 2 * me + frame)).astype(BF16)


def back_body(area, width, total_clips, length_ref, own, cot, later, wt_ref, gin_ref, grads):
    me = lax.axis_index("tm")
    height = area // width
    for frame in range(2):
        rows = slice(frame * area, (frame + 1) * area)
        for at, ref in ((frame, cot), (2 + frame, later)):
            value = ref[rows, :].astype(F32) * kept(length_ref, 2 * me + at)
            fill_padded(grads, at, value, width, height, -1)
    for frame in range(2):
        rows = slice(frame * area, (frame + 1) * area)
        total = jnp.zeros((area, gin_ref.shape[1]), F32)
        for time_tap in range(3):
            for row_tap in range(3):
                first = (2 - row_tap) * width
                window = grads[frame + 2 - time_tap, first : first + area, :]
                total = total + jnp.dot(
                    window, wt_ref[3 * time_tap + row_tap], preferred_element_type=F32
                )
        values = own[rows, :].astype(F32)
        sig = jax.nn.sigmoid(values)
        slope = sig * (1.0 + values * (1.0 - sig))
        keep = kept(length_ref, 2 * me + frame)
        gin_ref[rows, :] = (total * slope * (keep / total_clips)).astype(BF16)


def turn_body(w_ref, out_ref):
    wide = w_ref.shape[2]
    for tap in range(27):
        rows = slice(tap % 3 * wide, (tap % 3 + 1) * wide)
        out_ref[tap // 3, rows, :] = w_ref[tap // 3, rows, :].T


def local(video_clips, cotangent, weight, lengths):
    clip_count, frame_count, height, width, channels = video_clips.shape
    peers, shards = lax.axis_size("tm"), lax.axis_size("dp")
    total_clips = clip_count * shards
    area = height * width
    assert clip_count == 1 and frame_count == 2, "block shape"
    assert 2 * channels == peers * LANES and peers == 4, "tm size"
    clips = video_clips.reshape(2 * area, channels)
    cot = cotangent.reshape(2 * area, channels)

    block = (2 * area, channels)
    near_x, near_y = swaps([clips] * 2, "tm", 1)
    *slices, own = call(
        functools.partial(slice_body, peers, area),
        [pltpu.VMEM((area, LANES), BF16)] * peers + [pltpu.VMEM(block, BF16)],
        (cot, clips),
        resident=False,
        scratch=[
            pltpu.VMEM((channels // LANES, 2 * area, LANES), BF16),
            pltpu.VMEM((peers, area, LANES), F32),
            pltpu.SemaphoreType.DMA((channels // LANES + 1,)),
        ],
    )
    slices = [slices[0]] + swaps(slices[1:], "tm", 1)
    split = area + area // 4
    relayed = [
        call(functools.partial(cut_body, start), [pltpu.VMEM((size, channels), BF16)], (near,))[0]
        for start, size, near in ((0, split, near_x), (split, 2 * area - split, near_y))
    ]
    first = swap(relayed[0], "tm", 2)
    second = swap(relayed[1], "tm", 1)
    later = lax.ppermute(cot, "tm", [(s, s - 1) for s in range(1, peers)])
    (act_t,) = call(
        functools.partial(turn_blocks_body, area),
        [pltpu.VMEM((channels, 2 * peers * area), BF16)],
        (own, near_x, near_y),
    )
    (grads,) = call(
        functools.partial(place_grads_body, peers, area, width),
        [pltpu.VMEM((2 * (peers + 1) * area, 5 * LANES), BF16)],
        (lengths, *slices),
    )

    parts = shards // 2
    count = channels // shards
    lanes = 14 * LANES
    products = call(
        functools.partial(products_body, peers, area),
        [pltpu.VMEM((channels, 5 * LANES), F32)] * 3,
        (grads, act_t),
        flops=2 * 27 * 2 * peers * area * channels * LANES // 2,
    )
    keep, send = call(
        functools.partial(kernel_grad_body, area),
        [pltpu.VMEM((parts, count, lanes), F32), pltpu.VMEM((parts, count, lanes), BF16)],
        (grads, first, second, *products),
        flops=2 * 27 * 2 * area * channels * LANES // 2,
    )
    flat = weight.reshape(9, 3 * channels, channels)
    token = pltpu.VMEM((8, LANES), F32)
    padded = pltpu.VMEM((4, area + 2 * width, 3 * channels), BF16)
    flops = 2 * 27 * 2 * area * channels * channels
    conv_out, token_a = call(
        functools.partial(ahead_body, area, width),
        [sds(block, BF16), token],
        (lengths, own, near_x, first, second, flat),
        after=(keep,),
        scratch=[padded],
        flops=flops,
    )
    (turned,) = call(turn_body, [pltpu.VMEM(flat.shape, BF16)], (flat,), after=(token_a,))
    piece = sum_over_clips(keep, send, (token_a,))
    (input_grad,) = call(
        functools.partial(back_body, area, width, total_clips),
        [sds(block, BF16)],
        (lengths, own, cot, later, turned),
        after=(piece,),
        scratch=[padded],
        flops=flops,
    )
    pieces = [piece] + swaps([piece] * (peers - 1), "tm", 1)
    (placed,) = call(
        functools.partial(place_body, peers, 1.0 / total_clips),
        [sds((27, count, channels), F32)],
        pieces,
        scratch=[pltpu.VMEM((peers, count, lanes), F32)],
    )
    shape = video_clips.shape
    weight_grad = placed.reshape(3, 3, 3, count, channels)
    return conv_out.reshape(shape), input_grad.reshape(shape), weight_grad


def cuts(parts):
    found = []
    while parts > 1:
        if parts % 4 == 0:
            found.append(parts)
        parts //= 4 if parts % 4 == 0 else 2
    return found


def solution(mesh):
    in_specs = (P("dp", "tm", None, None, None), P("dp", "tm", None, None, None), P(), P("dp"))
    out_specs = (
        P("dp", "tm", None, None, None),
        P("dp", "tm", None, None, None),
        P(None, None, None, "dp", None),
    )

    program = jax.shard_map(local, mesh=mesh, in_specs=in_specs, out_specs=out_specs, check_vma=False)
    sizes = cuts(mesh.shape["dp"] // 2)
    assert sizes, "dp size"
    return program
```

```python
import functools

import jax
import jax.numpy as jnp
from jax import lax
from jax.experimental import pallas as pl
from jax.experimental.pallas import tpu as pltpu
from jax.sharding import PartitionSpec as P


F32 = jnp.float32
BF16 = jnp.bfloat16
LANES = 128
VMEM = pl.BlockSpec(memory_space=pltpu.VMEM)


def call(body, outs, args, *, after=(), resident=True, scratch=(), flops=0, aliases=None):
    moved = sum(a.size * a.dtype.itemsize for a in args)
    space = pltpu.VMEM if resident else pltpu.HBM
    held = [a if a.size == 1 else pltpu.with_memory_space_constraint(a, space) for a in args]
    count = len(args)

    def with_after(*refs):
        body(*refs[:count], *refs[count + len(after) :])

    return pl.pallas_call(
        with_after,
        out_shape=tuple(outs),
        in_specs=[pl.BlockSpec(memory_space=pltpu.SMEM if a.size == 1 else space) for a in args]
        + [pl.BlockSpec(memory_space=pl.ANY)] * len(after),
        out_specs=tuple(VMEM for _ in outs),
        scratch_shapes=list(scratch),
        input_output_aliases=aliases or {},
        compiler_params=pltpu.CompilerParams(vmem_limit_bytes=32 << 20),
        cost_estimate=pl.CostEstimate(flops=flops, bytes_accessed=moved, transcendentals=0),
    )(*held, *after)


def sds(shape, dtype):
    return jax.ShapeDtypeStruct(shape, dtype)


def swap(value, axis, mask):
    count = lax.axis_size(axis)
    return lax.ppermute(value, axis, [(s, s ^ mask) for s in range(count)])


def first_mask(core):
    return 1 + core


def cross(value, first):
    peers, shards = lax.axis_size("tm"), lax.axis_size("dp")
    pairs = []
    for t in range(peers):
        for d in range(shards):
            mask = first_mask(d % 2) if first else 3 - first_mask(d % 2)
            pairs.append((t * shards + d, (t ^ mask) * shards + d))
    return lax.ppermute(value, ("tm", "dp"), pairs)


def peer_block(turn):
    me = lax.axis_index("tm")
    if turn in (0, 3):
        return me ^ turn
    mask = first_mask(lax.axis_index("dp") % 2)
    return me ^ (mask if turn == 1 else 3 - mask)


def swaps(values, axis, step):
    got = []
    for m, value in enumerate(values):
        got.append(swap(value, axis, (m + 1) * step))
    return got


def low_half(shape):
    return lax.broadcasted_iota(jnp.int32, shape, len(shape) - 1) < LANES // 2


def half_turn(value):
    return pltpu.roll(value, LANES // 2, axis=1)


def column_shift(value, step, width):
    if step == 0:
        return value
    rows = value.shape[0]
    turned = pltpu.roll(value, (-step) % rows, axis=0)
    column = lax.broadcasted_iota(jnp.int32, value.shape, 0) % width
    edge = width - 1 if step > 0 else 0
    return jnp.where(column == edge, jnp.zeros_like(turned), turned)


def row_shift(value, step, width):
    if step == 0:
        return value
    blank = jnp.zeros((width, value.shape[1]), value.dtype)
    if step > 0:
        return jnp.concatenate([value[width:], blank], axis=0)
    return jnp.concatenate([blank, value[:-width]], axis=0)


def kept(length_ref, frame):
    return jnp.where(frame < length_ref[0], 1.0, 0.0).astype(F32)


def slice_body(peers, area, cot_hbm, clips_hbm, *refs):
    outs, own = refs[:peers], refs[peers]
    cot, picks, sems = refs[peers + 1 :]
    copies = []
    for tile in range(cot.shape[0]):
        lanes = pl.ds(tile * LANES, LANES)
        copies.append(pltpu.make_async_copy(cot_hbm.at[:, lanes], cot.at[tile], sems.at[tile]))
    own_copy = pltpu.make_async_copy(clips_hbm, own, sems.at[len(copies)])
    for copy in (*copies, own_copy):
        copy.start()
    low = low_half((area, LANES))
    halves = peers // len(copies)
    for tile, copy in enumerate(copies):
        copy.wait()
        first = cot[tile, :area, :].astype(F32)
        second = cot[tile, area:, :].astype(F32)
        picks[tile * halves] = jnp.where(low, first, half_turn(second))
        picks[tile * halves + 1] = jnp.where(low, half_turn(first), second)
    for turn, out in enumerate(outs):
        out[...] = picks[peer_block(turn)].astype(BF16)
    own_copy.wait()


def place_slice(area, width, length_ref, block, slice_ref, grads):
    low = low_half((area, LANES))
    start = pl.multiple_of(block * 2 * area, 2 * area)
    keep = jnp.where(low, kept(length_ref, 2 * block), kept(length_ref, 2 * block + 1))
    both = slice_ref[...].astype(F32) * keep
    taps = []
    for row_tap in range(3):
        for col_tap in range(3):
            moved = column_shift(both, 1 - col_tap, width)
            turned = half_turn(moved)
            taps.append([row_shift(v, 1 - row_tap, width) for v in (moved, turned)])
    taps.append([jnp.zeros_like(both)] * 2)
    for tile in range(5):
        (even, even_turned), (odd, odd_turned) = taps[2 * tile], taps[2 * tile + 1]
        for frame in range(2):
            left, right = (even, odd_turned) if frame == 0 else (even_turned, odd)
            grads[pl.ds(start + frame * area, area), tile * LANES : (tile + 1) * LANES] = (
                jnp.where(low, left, right).astype(BF16)
            )


def place_grads_body(masks, area, width, length_ref, *refs):
    slices, grads = refs[: len(masks)], refs[-1]
    grads[grads.shape[0] - 2 * area :, :] = jnp.zeros((2 * area, grads.shape[1]), BF16)
    for mask, ref in zip(masks, slices):
        place_slice(area, width, length_ref, peer_block(mask), ref, grads)


def cut_body(start, source, out_ref):
    out_ref[...] = source[start : start + out_ref.shape[0], :]


def turn_frame(act_t, block, frame, values):
    area = values.shape[0]
    at = pl.multiple_of((2 * block + frame) * area, area)
    act_t[:, pl.ds(at, area)] = jax.nn.silu(values.astype(F32)).astype(BF16).T


def turn_blocks_body(area, *refs):
    act_t = refs[-1]
    me = lax.axis_index("tm")
    for mask, ref in enumerate(refs[:-1]):
        for frame in range(2):
            turn_frame(act_t, peer_block(mask), frame, ref[frame * area : (frame + 1) * area, :])
    at = pl.multiple_of(2 * (me ^ 3) * area, area)
    act_t[:, pl.ds(at, 2 * area)] = jnp.zeros((act_t.shape[0], 2 * area), BF16)


def products_body(peers, masks, area, width, length_ref, *refs):
    slices, near_b = refs[: len(masks)], refs[len(masks)]
    grads, act_t, *outs = refs[len(masks) + 3 :]
    block = peer_block(2)
    for mask, ref in zip(masks, slices):
        place_slice(area, width, length_ref, peer_block(mask), ref, grads)
    for frame in range(2):
        turn_frame(act_t, block, frame, near_b[frame * area : (frame + 1) * area, :])
    for time_tap, out in enumerate(outs):
        used = (2 * peers - 2 + time_tap) * area
        first = (2 - time_tap) * area
        out[...] = jnp.dot(
            act_t[:, :used], grads[first : first + used, :], preferred_element_type=F32
        )


def kernel_grad_body(area, grads, first, second, *refs):
    held, (keep_ref, send_ref) = refs[:3], refs[3:]
    me = lax.axis_index("tm")
    core = lax.axis_index("dp") % 2
    values = jnp.concatenate([first[...], second[...]], axis=0).astype(F32)
    turned = jax.nn.silu(values).astype(BF16).T
    sums = []
    for time_tap, ref in enumerate(held):
        at = pl.multiple_of((2 * (me ^ 3) + 2 - time_tap) * area, area)
        sums.append(
            ref[...]
            + jnp.dot(turned, grads[pl.ds(at, 2 * area), :], preferred_element_type=F32)
        )
    tiles = [s[:, tile * LANES : (tile + 1) * LANES] for s in sums for tile in range(4)]
    last = [s[:, 4 * LANES :] for s in sums]
    low = low_half(last[0].shape)
    tiles.append(jnp.where(low, last[0], half_turn(last[1])))
    tiles.append(last[2])
    parts, count = keep_ref.shape[:2]
    groups = [
        [t[(2 * z + c) * count : (2 * z + c + 1) * count] for t in tiles]
        for z in range(parts)
        for c in range(2)
    ]
    for own in range(2):

        @pl.when(core == own)
        def _(own=own):
            for z in range(parts):
                for at in range(len(tiles)):
                    lanes = slice(at * LANES, (at + 1) * LANES)
                    keep_ref[z, :, lanes] = groups[2 * z + own][at]
                    send_ref[z, :, lanes] = groups[2 * z + 1 - own][at].astype(BF16)


def sum_body(arrived, radix, step, *refs):
    keep_ref, in_refs = refs[0], refs[1 : 1 + arrived]
    total = keep_ref[...]
    for ref in in_refs:
        total = total + ref[...].astype(F32)
    if radix == 1:
        refs[1 + arrived][...] = total[0].astype(BF16)
        return
    out_refs, held = refs[1 + arrived : -1], refs[-1]
    held[...] = total
    digit = (lax.axis_index("dp") // 2) // step % radix
    for mask, out in enumerate(out_refs):
        out[...] = held[pl.ds((digit ^ mask) * step, step)].astype(out.dtype)


def sum_over_clips(keep, send, after):
    arrived = [swap(send, "dp", 1)]
    while True:
        parts, count, lanes = keep.shape
        radix = 1 if parts == 1 else (4 if parts % 4 == 0 else 2)
        assert parts % radix == 0 and radix & (radix - 1) == 0, "dp size"
        step = parts // radix
        if radix == 1:
            return call(
                functools.partial(sum_body, len(arrived), 1, 1),
                [pltpu.VMEM((count, lanes), BF16)],
                (keep, *arrived),
                after=after,
            )[0]
        outs = [pltpu.VMEM((step, count, lanes), F32)]
        outs += [pltpu.VMEM((step, count, lanes), BF16)] * (radix - 1)
        keep, *sends = call(
            functools.partial(sum_body, len(arrived), radix, step),
            outs,
            (keep, *arrived),
            scratch=[pltpu.VMEM((parts, count, lanes), F32)],
        )
        arrived = swaps(sends, "dp", 2 * step)


def place_body(peers, scale, *refs):
    pieces, out_ref, held = refs[:peers], refs[peers], refs[peers + 1]
    me = lax.axis_index("tm")
    for mask, piece in enumerate(pieces):
        held[me ^ mask] = piece[...].astype(F32) * scale
    low = low_half((held.shape[1], LANES))
    for time_tap in range(3):
        for tap in range(9):
            tile = 4 * time_tap + tap // 2 if tap < 8 else 12 + time_tap // 2
            half = tap % 2 if tap < 8 else time_tap % 2
            for pair in range(peers // 2):
                left = held[2 * pair, :, tile * LANES : (tile + 1) * LANES]
                right = held[2 * pair + 1, :, tile * LANES : (tile + 1) * LANES]
                if half == 0:
                    value = jnp.where(low, left, half_turn(right))
                else:
                    value = jnp.where(low, half_turn(left), right)
                out_ref[9 * time_tap + tap, :, pair * LANES : (pair + 1) * LANES] = value


def fill_padded(out_ref, frame, value, width, height, direction):
    wide = value.shape[1]
    blank = jnp.zeros((width, 3 * wide), BF16)
    out_ref[frame, :width, :] = blank
    out_ref[frame, (height + 1) * width :, :] = blank
    for tap in range(3):
        out_ref[frame, width : (height + 1) * width, tap * wide : (tap + 1) * wide] = column_shift(
            value, direction * (tap - 1), width
        ).astype(BF16)


def ahead_body(area, width, length_ref, own, near_a, near_b, first, second, w_ref, *refs):
    out_ref, token_ref, acts = refs
    token_ref[...] = jnp.zeros_like(token_ref)
    me = lax.axis_index("tm")
    height = area // width
    far = jnp.concatenate([first[...], second[...]], axis=0)
    for frame in range(2):
        rows = slice(frame * area, (frame + 1) * area)
        value = jnp.zeros((area, far.shape[1]), F32)
        for turn, block in ((1, near_a[rows, :]), (2, near_b[rows, :]), (3, far[rows])):
            value = jnp.where(peer_block(turn) == me - 1, block.astype(F32), value)
        fill_padded(acts, frame, jax.nn.silu(value), width, height, 1)
        value = own[rows, :].astype(F32)
        fill_padded(acts, 2 + frame, jax.nn.silu(value), width, height, 1)
    for frame in range(2):
        rows = slice(frame * area, (frame + 1) * area)
        total = jnp.zeros((area, out_ref.shape[1]), F32)
        for time_tap in range(3):
            for row_tap in range(3):
                window = acts[frame + time_tap, row_tap * width : row_tap * width + area, :]
                total = total + jnp.dot(
                    window, w_ref[3 * time_tap + row_tap], preferred_element_type=F32
                )
        out_ref[rows, :] = (total * kept(length_ref, 2 * me + frame)).astype(BF16)


def back_body(area, width, total_clips, length_ref, own, cot, later, wt_ref, gin_ref, grads):
    me = lax.axis_index("tm")
    height = area // width
    for frame in range(2):
        rows = slice(frame * area, (frame + 1) * area)
        for at, ref in ((frame, cot), (2 + frame, later)):
            value = ref[rows, :].astype(F32) * kept(length_ref, 2 * me + at)
            fill_padded(grads, at, value, width, height, -1)
    for frame in range(2):
        rows = slice(frame * area, (frame + 1) * area)
        total = jnp.zeros((area, gin_ref.shape[1]), F32)
        for time_tap in range(3):
            for row_tap in range(3):
                first = (2 - row_tap) * width
                window = grads[frame + 2 - time_tap, first : first + area, :]
                total = total + jnp.dot(
                    window, wt_ref[3 * time_tap + row_tap], preferred_element_type=F32
                )
        values = own[rows, :].astype(F32)
        sig = jax.nn.sigmoid(values)
        slope = sig * (1.0 + values * (1.0 - sig))
        keep = kept(length_ref, 2 * me + frame)
        gin_ref[rows, :] = (total * slope * (keep / total_clips)).astype(BF16)


def turn_body(w_ref, out_ref):
    wide = w_ref.shape[2]
    for tap in range(27):
        rows = slice(tap % 3 * wide, (tap % 3 + 1) * wide)
        out_ref[tap // 3, rows, :] = w_ref[tap // 3, rows, :].T


def local(video_clips, cotangent, weight, lengths):
    clip_count, frame_count, height, width, channels = video_clips.shape
    peers, shards = lax.axis_size("tm"), lax.axis_size("dp")
    total_clips = clip_count * shards
    area = height * width
    assert clip_count == 1 and frame_count == 2, "block shape"
    assert 2 * channels == peers * LANES and peers == 4, "tm size"
    clips = video_clips.reshape(2 * area, channels)
    cot = cotangent.reshape(2 * area, channels)

    block = (2 * area, channels)
    near_a = cross(clips, True)
    near_b = cross(clips, False)
    *slices, own = call(
        functools.partial(slice_body, peers, area),
        [pltpu.VMEM((area, LANES), BF16)] * peers + [pltpu.VMEM(block, BF16)],
        (cot, clips),
        resident=False,
        scratch=[
            pltpu.VMEM((channels // LANES, 2 * area, LANES), BF16),
            pltpu.VMEM((peers, area, LANES), F32),
            pltpu.SemaphoreType.DMA((channels // LANES + 1,)),
        ],
    )
    slices[1] = cross(slices[1], True)
    slices[2] = cross(slices[2], False)
    slices[3] = swap(slices[3], "tm", 3)
    split = area + area // 4
    relayed = [
        call(functools.partial(cut_body, start), [pltpu.VMEM((size, channels), BF16)], (near,))[0]
        for start, size, near in ((0, split, near_a), (split, 2 * area - split, near_b))
    ]
    first = cross(relayed[0], False)
    second = cross(relayed[1], True)
    later = lax.ppermute(cot, "tm", [(s, s - 1) for s in range(1, peers)])
    (act_t,) = call(
        functools.partial(turn_blocks_body, area),
        [pltpu.VMEM((channels, 2 * peers * area), BF16)],
        (own, near_a),
    )
    (grads,) = call(
        functools.partial(place_grads_body, (0, 1,), area, width),
        [pltpu.VMEM((2 * (peers + 1) * area, 5 * LANES), BF16)],
        (lengths, slices[0], slices[1]),
    )

    parts = shards // 2
    count = channels // shards
    lanes = 14 * LANES
    grads, _, *products = call(
        functools.partial(products_body, peers, (3, 2,), area, width),
        [pltpu.VMEM(grads.shape, BF16), pltpu.VMEM(act_t.shape, BF16)]
        + [pltpu.VMEM((channels, 5 * LANES), F32)] * 3,
        (lengths, slices[3], slices[2], near_b, grads, act_t),
        aliases={4: 0, 5: 1},
        flops=2 * 27 * 2 * peers * area * channels * LANES // 2,
    )
    keep, send = call(
        functools.partial(kernel_grad_body, area),
        [pltpu.VMEM((parts, count, lanes), F32), pltpu.VMEM((parts, count, lanes), BF16)],
        (grads, first, second, *products),
        flops=2 * 27 * 2 * area * channels * LANES // 2,
    )
    flat = weight.reshape(9, 3 * channels, channels)
    token = pltpu.VMEM((8, LANES), F32)
    padded = pltpu.VMEM((4, area + 2 * width, 3 * channels), BF16)
    flops = 2 * 27 * 2 * area * channels * channels
    conv_out, token_a = call(
        functools.partial(ahead_body, area, width),
        [sds(block, BF16), token],
        (lengths, own, near_a, near_b, first, second, flat),
        after=(keep,),
        scratch=[padded],
        flops=flops,
    )
    (turned,) = call(turn_body, [pltpu.VMEM(flat.shape, BF16)], (flat,), after=(token_a,))
    piece = sum_over_clips(keep, send, (token_a,))
    (input_grad,) = call(
        functools.partial(back_body, area, width, total_clips),
        [sds(block, BF16)],
        (lengths, own, cot, later, turned),
        after=(piece,),
        scratch=[padded],
        flops=flops,
    )
    pieces = [piece] + swaps([piece] * (peers - 1), "tm", 1)
    (placed,) = call(
        functools.partial(place_body, peers, 1.0 / total_clips),
        [sds((27, count, channels), F32)],
        pieces,
        scratch=[pltpu.VMEM((peers, count, lanes), F32)],
    )
    shape = video_clips.shape
    weight_grad = placed.reshape(3, 3, 3, count, channels)
    return conv_out.reshape(shape), input_grad.reshape(shape), weight_grad


def cuts(parts):
    found = []
    while parts > 1:
        if parts % 4 == 0:
            found.append(parts)
        parts //= 4 if parts % 4 == 0 else 2
    return found


def solution(mesh):
    in_specs = (P("dp", "tm", None, None, None), P("dp", "tm", None, None, None), P(), P("dp"))
    out_specs = (
        P("dp", "tm", None, None, None),
        P("dp", "tm", None, None, None),
        P(None, None, None, "dp", None),
    )

    program = jax.shard_map(local, mesh=mesh, in_specs=in_specs, out_specs=out_specs, check_vma=False)
    sizes = cuts(mesh.shape["dp"] // 2)
    assert sizes, "dp size"
    return program
```

```python
import functools

import jax
import jax.numpy as jnp
from jax import lax
from jax.experimental import pallas as pl
from jax.experimental.pallas import tpu as pltpu
from jax.sharding import PartitionSpec as P


F32 = jnp.float32
BF16 = jnp.bfloat16
LANES = 128


def call(
    body, outs, args, *, after=(), resident=True, scratch=(), flops=0, aliases=None,
    out_space=pltpu.VMEM,
):
    moved = sum(a.size * a.dtype.itemsize for a in args)
    space = pltpu.VMEM if resident else pltpu.HBM
    held = [a if a.size == 1 else pltpu.with_memory_space_constraint(a, space) for a in args]
    count = len(args)

    def with_after(*refs):
        body(*refs[:count], *refs[count + len(after) :])

    return pl.pallas_call(
        with_after,
        out_shape=tuple(outs),
        in_specs=[pl.BlockSpec(memory_space=pltpu.SMEM if a.size == 1 else space) for a in args]
        + [pl.BlockSpec(memory_space=pl.ANY)] * len(after),
        out_specs=tuple(pl.BlockSpec(memory_space=out_space) for _ in outs),
        scratch_shapes=list(scratch),
        input_output_aliases=aliases or {},
        compiler_params=pltpu.CompilerParams(vmem_limit_bytes=32 << 20),
        cost_estimate=pl.CostEstimate(flops=flops, bytes_accessed=moved, transcendentals=0),
    )(*held, *after)


def sds(shape, dtype):
    return jax.ShapeDtypeStruct(shape, dtype)


def swap(value, axis, mask):
    count = lax.axis_size(axis)
    return lax.ppermute(value, axis, [(s, s ^ mask) for s in range(count)])


def first_mask(core):
    return 1 + core


def cross(value, first):
    peers, shards = lax.axis_size("tm"), lax.axis_size("dp")
    pairs = []
    for t in range(peers):
        for d in range(shards):
            mask = first_mask(d % 2) if first else 3 - first_mask(d % 2)
            pairs.append((t * shards + d, (t ^ mask) * shards + d))
    return lax.ppermute(value, ("tm", "dp"), pairs)


def peer_block(turn):
    me = lax.axis_index("tm")
    if turn in (0, 3):
        return me ^ turn
    mask = first_mask(lax.axis_index("dp") % 2)
    return me ^ (mask if turn == 1 else 3 - mask)


def swaps(values, axis, step):
    got = []
    for m, value in enumerate(values):
        got.append(swap(value, axis, (m + 1) * step))
    return got


def low_half(shape):
    return lax.broadcasted_iota(jnp.int32, shape, len(shape) - 1) < LANES // 2


def half_turn(value):
    return pltpu.roll(value, LANES // 2, axis=1)


def column_shift(value, step, width):
    if step == 0:
        return value
    rows = value.shape[0]
    turned = pltpu.roll(value, (-step) % rows, axis=0)
    column = lax.broadcasted_iota(jnp.int32, value.shape, 0) % width
    edge = width - 1 if step > 0 else 0
    return jnp.where(column == edge, jnp.zeros_like(turned), turned)


def row_shift(value, step, width):
    if step == 0:
        return value
    blank = jnp.zeros((width, value.shape[1]), value.dtype)
    if step > 0:
        return jnp.concatenate([value[width:], blank], axis=0)
    return jnp.concatenate([blank, value[:-width]], axis=0)


def kept(length_ref, frame):
    return jnp.where(frame < length_ref[0], 1.0, 0.0).astype(F32)


def slice_body(peers, area, cot_hbm, clips_hbm, *refs):
    outs, own = refs[:peers], refs[peers]
    cot, picks, sems = refs[peers + 1 :]
    copies = []
    for tile in range(cot.shape[0]):
        lanes = pl.ds(tile * LANES, LANES)
        copies.append(pltpu.make_async_copy(cot_hbm.at[:, lanes], cot.at[tile], sems.at[tile]))
    own_copy = pltpu.make_async_copy(clips_hbm, own, sems.at[len(copies)])
    for copy in (*copies, own_copy):
        copy.start()
    low = low_half((area, LANES))
    halves = peers // len(copies)
    for tile, copy in enumerate(copies):
        copy.wait()
        first = cot[tile, :area, :].astype(F32)
        second = cot[tile, area:, :].astype(F32)
        picks[tile * halves] = jnp.where(low, first, half_turn(second))
        picks[tile * halves + 1] = jnp.where(low, half_turn(first), second)
    for turn, out in enumerate(outs):
        out[...] = picks[peer_block(turn)].astype(BF16)
    own_copy.wait()


def place_slice(area, width, length_ref, block, slice_ref, grads):
    low = low_half((area, LANES))
    start = pl.multiple_of(block * 2 * area, 2 * area)
    keep = jnp.where(low, kept(length_ref, 2 * block), kept(length_ref, 2 * block + 1))
    both = slice_ref[...].astype(F32) * keep
    taps = []
    for row_tap in range(3):
        for col_tap in range(3):
            moved = column_shift(both, 1 - col_tap, width)
            turned = half_turn(moved)
            taps.append([row_shift(v, 1 - row_tap, width) for v in (moved, turned)])
    taps.append([jnp.zeros_like(both)] * 2)
    for tile in range(5):
        (even, even_turned), (odd, odd_turned) = taps[2 * tile], taps[2 * tile + 1]
        for frame in range(2):
            left, right = (even, odd_turned) if frame == 0 else (even_turned, odd)
            grads[pl.ds(start + frame * area, area), tile * LANES : (tile + 1) * LANES] = (
                jnp.where(low, left, right).astype(BF16)
            )


def cut_body(start, source, out_ref):
    out_ref[...] = source[start : start + out_ref.shape[0], :]


def turn_frame(act_t, turn, frame, values):
    area = values.shape[0]
    at = (2 * turn + frame) * area
    act_t[:, at : at + area] = jax.nn.silu(values.astype(F32)).astype(BF16).T


def turn_block(area, act_t, turn, ref):
    for frame in range(2):
        turn_frame(act_t, turn, frame, ref[frame * area : (frame + 1) * area, :])


def own_body(area, width, length_ref, own, slice_ref, act_t, grads):
    turn_block(area, act_t, 0, own)
    grads[grads.shape[0] - 2 * area :, :] = jnp.zeros((2 * area, grads.shape[1]), BF16)
    place_slice(area, width, length_ref, lax.axis_index("tm"), slice_ref, grads)


def windows(area, grads, turn, time_tap):
    at = pl.multiple_of((2 * peer_block(turn) + 2 - time_tap) * area, area)
    return grads[pl.ds(at, 2 * area), :]


def near_body(area, width, length_ref, slice_a, near_a, near_b, *refs):
    grads, act_t = refs[2:]
    place_slice(area, width, length_ref, peer_block(1), slice_a, grads)
    turn_block(area, act_t, 1, near_a)
    turn_block(area, act_t, 2, near_b)


def products_body(area, width, length_ref, slice_b, slice_3, act_t, _, grads, *outs):
    for turn, ref in ((2, slice_b), (3, slice_3)):
        place_slice(area, width, length_ref, peer_block(turn), ref, grads)
    for time_tap, out in enumerate(outs):
        used = [windows(area, grads, turn, time_tap) for turn in range(3)]
        out[...] = jnp.dot(
            act_t[...], jnp.concatenate(used, axis=0), preferred_element_type=F32
        )


def sums_shape(parts, count):
    if count % 32 == 0:
        return (parts, 13 * count + count // 2, LANES)
    return (parts, count, 14 * LANES)


def put_tile(ref, part, tile, value):
    count = value.shape[0]
    if ref.shape[2] != LANES:
        ref[part, :, tile * LANES : (tile + 1) * LANES] = value
        return
    if tile == 13:
        low = low_half((count // 2, LANES))
        value = jnp.where(low, value[: count // 2], half_turn(value[count // 2 :]))
    ref[part, tile * count : tile * count + value.shape[0], :] = value


def get_tile(ref, part, tile, count):
    if ref.shape[2] != LANES:
        return ref[part, :, tile * LANES : (tile + 1) * LANES]
    if tile < 13:
        return ref[part, tile * count : (tile + 1) * count, :]
    value = ref[part, tile * count :, :]
    return jnp.concatenate([value, half_turn(value)], axis=0)


def kernel_grad_body(count, area, grads, first, second, *refs):
    held, (keep_ref, send_ref) = refs[:3], refs[3:]
    core = lax.axis_index("dp") % 2
    values = jnp.concatenate([first[...], second[...]], axis=0).astype(F32)
    turned = jax.nn.silu(values).astype(BF16).T
    sums = []
    for time_tap, ref in enumerate(held):
        sums.append(
            ref[...]
            + jnp.dot(turned, windows(area, grads, 3, time_tap), preferred_element_type=F32)
        )
    tiles = [s[:, tile * LANES : (tile + 1) * LANES] for s in sums for tile in range(4)]
    last = [s[:, 4 * LANES :] for s in sums]
    low = low_half(last[0].shape)
    tiles.append(jnp.where(low, last[0], half_turn(last[1])))
    tiles.append(last[2])
    parts = keep_ref.shape[0]
    groups = [
        [t[(2 * z + c) * count : (2 * z + c + 1) * count] for t in tiles]
        for z in range(parts)
        for c in range(2)
    ]
    for own in range(2):

        @pl.when(core == own)
        def _(own=own):
            for z in range(parts):
                for at in range(len(tiles)):
                    put_tile(keep_ref, z, at, groups[2 * z + own][at])
                    put_tile(send_ref, z, at, groups[2 * z + 1 - own][at].astype(BF16))


def sum_body(arrived, radix, step, *refs):
    keep_ref, in_refs = refs[0], refs[1 : 1 + arrived]
    total = keep_ref[...]
    for ref in in_refs:
        total = total + ref[...].astype(F32)
    if radix == 1:
        refs[1 + arrived][...] = total[0].astype(BF16)
        return
    out_refs, held = refs[1 + arrived : -1], refs[-1]
    held[...] = total
    digit = (lax.axis_index("dp") // 2) // step % radix
    for mask, out in enumerate(out_refs):
        out[...] = held[pl.ds((digit ^ mask) * step, step)].astype(out.dtype)


def sum_over_clips(keep, send, after):
    arrived = [swap(send, "dp", 1)]
    while True:
        parts, count, lanes = keep.shape
        radix = 1 if parts == 1 else (4 if parts % 4 == 0 else 2)
        assert parts % radix == 0 and radix & (radix - 1) == 0, "dp size"
        step = parts // radix
        if radix == 1:
            return call(
                functools.partial(sum_body, len(arrived), 1, 1),
                [pltpu.VMEM((count, lanes), BF16)],
                (keep, *arrived),
                after=after,
            )[0]
        outs = [pltpu.VMEM((step, count, lanes), F32)]
        outs += [pltpu.VMEM((step, count, lanes), BF16)] * (radix - 1)
        keep, *sends = call(
            functools.partial(sum_body, len(arrived), radix, step),
            outs,
            (keep, *arrived),
            scratch=[pltpu.VMEM((parts, count, lanes), F32)],
        )
        arrived = swaps(sends, "dp", 2 * step)


def place_body(peers, scale, *refs):
    pieces, out_hbm, held, placed, sems = refs[:peers], *refs[peers:]
    for turn, piece in enumerate(pieces):
        held[lax.axis_index("tm") ^ turn] = piece[...].astype(F32) * scale
    count = placed.shape[1]
    low = low_half((count, LANES))
    copies = []
    for time_tap in range(3):
        for tap in range(9):
            tile = 4 * time_tap + tap // 2 if tap < 8 else 12 + time_tap // 2
            half = tap % 2 if tap < 8 else time_tap % 2
            for pair in range(peers // 2):
                left = get_tile(held, 2 * pair, tile, count)
                right = get_tile(held, 2 * pair + 1, tile, count)
                if half == 0:
                    value = jnp.where(low, left, half_turn(right))
                else:
                    value = jnp.where(low, half_turn(left), right)
                placed[9 * time_tap + tap, :, pair * LANES : (pair + 1) * LANES] = value
        taps = pl.ds(9 * time_tap, 9)
        copies.append(pltpu.make_async_copy(placed.at[taps], out_hbm.at[taps], sems.at[time_tap]))
        copies[-1].start()
    for copy in copies:
        copy.wait()


def fill_padded(out_ref, frame, value, width, height, direction):
    wide = value.shape[1]
    blank = jnp.zeros((width, 3 * wide), BF16)
    out_ref[frame, :width, :] = blank
    out_ref[frame, (height + 1) * width :, :] = blank
    for tap in range(3):
        out_ref[frame, width : (height + 1) * width, tap * wide : (tap + 1) * wide] = column_shift(
            value, direction * (tap - 1), width
        ).astype(BF16)


def turn_taps(w_ref, out_ref, at):
    wide = w_ref.shape[2]
    for tap in range(3):
        rows = slice(tap * wide, (tap + 1) * wide)
        out_ref[at, rows, :] = w_ref[at, rows, :].T


def ahead_body(area, width, length_ref, own, near_a, near_b, first, second, w_ref, *refs):
    out_ref, token_ref, turned_ref, acts = refs
    token_ref[...] = jnp.zeros_like(token_ref)
    me = lax.axis_index("tm")
    height = area // width
    far = jnp.concatenate([first[...], second[...]], axis=0)
    for frame in range(2):
        rows = slice(frame * area, (frame + 1) * area)
        value = jnp.zeros((area, far.shape[1]), F32)
        for turn, block in ((1, near_a[rows, :]), (2, near_b[rows, :]), (3, far[rows])):
            value = jnp.where(peer_block(turn) == me - 1, block.astype(F32), value)
        fill_padded(acts, frame, jax.nn.silu(value), width, height, 1)
        value = own[rows, :].astype(F32)
        fill_padded(acts, 2 + frame, jax.nn.silu(value), width, height, 1)
    for frame in range(2):
        rows = slice(frame * area, (frame + 1) * area)
        total = jnp.zeros((area, out_ref.shape[1]), F32)
        for time_tap in range(3):
            for row_tap in range(3):
                window = acts[frame + time_tap, row_tap * width : row_tap * width + area, :]
                at = 3 * time_tap + row_tap
                total = total + jnp.dot(window, w_ref[at], preferred_element_type=F32)
                if frame == 0:
                    turn_taps(w_ref, turned_ref, at)
        out_ref[rows, :] = (total * kept(length_ref, 2 * me + frame)).astype(BF16)


def back_body(area, width, total_clips, length_ref, own, cot, later, wt_ref, gin_ref, grads):
    me = lax.axis_index("tm")
    height = area // width
    for frame in range(2):
        rows = slice(frame * area, (frame + 1) * area)
        for at, ref in ((frame, cot), (2 + frame, later)):
            value = ref[rows, :].astype(F32) * kept(length_ref, 2 * me + at)
            fill_padded(grads, at, value, width, height, -1)
    for frame in range(2):
        rows = slice(frame * area, (frame + 1) * area)
        total = jnp.zeros((area, gin_ref.shape[1]), F32)
        for time_tap in range(3):
            for row_tap in range(3):
                first = (2 - row_tap) * width
                window = grads[frame + 2 - time_tap, first : first + area, :]
                total = total + jnp.dot(
                    window, wt_ref[3 * time_tap + row_tap], preferred_element_type=F32
                )
        values = own[rows, :].astype(F32)
        sig = jax.nn.sigmoid(values)
        slope = sig * (1.0 + values * (1.0 - sig))
        keep = kept(length_ref, 2 * me + frame)
        gin_ref[rows, :] = (total * slope * (keep / total_clips)).astype(BF16)


def local(video_clips, cotangent, weight, lengths):
    clip_count, frame_count, height, width, channels = video_clips.shape
    peers, shards = lax.axis_size("tm"), lax.axis_size("dp")
    total_clips = clip_count * shards
    area = height * width
    assert clip_count == 1 and frame_count == 2, "block shape"
    assert 2 * channels == peers * LANES and peers == 4, "tm size"
    clips = video_clips.reshape(2 * area, channels)
    cot = cotangent.reshape(2 * area, channels)

    block = (2 * area, channels)
    near_a = cross(clips, True)
    near_b = cross(clips, False)
    *slices, own = call(
        functools.partial(slice_body, peers, area),
        [pltpu.VMEM((area, LANES), BF16)] * peers + [pltpu.VMEM(block, BF16)],
        (cot, clips),
        resident=False,
        scratch=[
            pltpu.VMEM((channels // LANES, 2 * area, LANES), BF16),
            pltpu.VMEM((peers, area, LANES), F32),
            pltpu.SemaphoreType.DMA((channels // LANES + 1,)),
        ],
    )
    slices[1] = cross(slices[1], True)
    slices[2] = cross(slices[2], False)
    slices[3] = swap(slices[3], "tm", 3)
    split = area
    relayed = [
        call(functools.partial(cut_body, start), [pltpu.VMEM((size, channels), BF16)], (near,))[0]
        for start, size, near in ((0, split, near_a), (split, 2 * area - split, near_b))
    ]
    first = cross(relayed[0], False)
    second = cross(relayed[1], True)
    later = lax.ppermute(cot, "tm", [(s, s - 1) for s in range(1, peers)])
    moved = pltpu.VMEM((2 * (peers + 1) * area, 5 * LANES), BF16)
    turned_acts = pltpu.VMEM((channels, 6 * area), BF16)
    act_t, grads = call(
        functools.partial(own_body, area, width), [turned_acts, moved], (lengths, own, slices[0])
    )
    parts = shards // 2
    count = channels // shards
    grads, act_t = call(
        functools.partial(near_body, area, width),
        [moved, turned_acts],
        (lengths, slices[1], near_a, near_b, grads, act_t),
        aliases={4: 0, 5: 1},
    )
    grads, *products = call(
        functools.partial(products_body, area, width),
        [moved] + [pltpu.VMEM((channels, 5 * LANES), F32)] * 3,
        (lengths, slices[2], slices[3], act_t, grads),
        aliases={4: 0},
        flops=2 * 27 * 2 * peers * area * channels * LANES // 2,
    )
    keep, send = call(
        functools.partial(kernel_grad_body, count, area),
        [pltpu.VMEM(sums_shape(parts, count), kind) for kind in (F32, BF16)],
        (grads, first, second, *products),
        flops=2 * 27 * 2 * area * channels * LANES // 2,
    )
    flat = weight.reshape(9, 3 * channels, channels)
    token = pltpu.VMEM((8, LANES), F32)
    padded = pltpu.VMEM((4, area + 2 * width, 3 * channels), BF16)
    flops = 2 * 27 * 2 * area * channels * channels
    conv_out, token_a, turned = call(
        functools.partial(ahead_body, area, width),
        [sds(block, BF16), token, pltpu.VMEM(flat.shape, BF16)],
        (lengths, own, near_a, near_b, first, second, flat),
        after=(keep,),
        scratch=[padded],
        flops=flops,
    )
    piece = sum_over_clips(keep, send, (token_a,))
    (input_grad,) = call(
        functools.partial(back_body, area, width, total_clips),
        [sds(block, BF16)],
        (lengths, own, cot, later, turned),
        after=(piece,),
        scratch=[padded],
        flops=flops,
    )
    pieces = [piece] + swaps([piece] * (peers - 1), "tm", 1)
    (placed,) = call(
        functools.partial(place_body, peers, 1.0 / total_clips),
        [sds((27, count, channels), F32)],
        pieces,
        scratch=[
            pltpu.VMEM((peers, *piece.shape), F32),
            pltpu.VMEM((27, count, channels), F32),
            pltpu.SemaphoreType.DMA((3,)),
        ],
        out_space=pl.ANY,
    )
    shape = video_clips.shape
    weight_grad = placed.reshape(3, 3, 3, count, channels)
    return conv_out.reshape(shape), input_grad.reshape(shape), weight_grad


def cuts(parts):
    found = []
    while parts > 1:
        if parts % 4 == 0:
            found.append(parts)
        parts //= 4 if parts % 4 == 0 else 2
    return found


def solution(mesh):
    in_specs = (P("dp", "tm", None, None, None), P("dp", "tm", None, None, None), P(), P("dp"))
    out_specs = (
        P("dp", "tm", None, None, None),
        P("dp", "tm", None, None, None),
        P(None, None, None, "dp", None),
    )

    program = jax.shard_map(local, mesh=mesh, in_specs=in_specs, out_specs=out_specs, check_vma=False)
    sizes = cuts(mesh.shape["dp"] // 2)
    assert sizes, "dp size"
    return program
```

```python
import functools

import jax
import jax.numpy as jnp
from jax import lax
from jax.experimental import pallas as pl
from jax.experimental.pallas import tpu as pltpu
from jax.sharding import PartitionSpec as P


F32 = jnp.float32
BF16 = jnp.bfloat16
LANES = 128


def call(
    body, outs, args, *, after=(), resident=True, scratch=(), flops=0, aliases=None,
    out_space=pltpu.VMEM,
):
    moved = sum(a.size * a.dtype.itemsize for a in args)
    space = pltpu.VMEM if resident else pltpu.HBM
    held = [a if a.size == 1 else pltpu.with_memory_space_constraint(a, space) for a in args]
    count = len(args)

    def with_after(*refs):
        body(*refs[:count], *refs[count + len(after) :])

    return pl.pallas_call(
        with_after,
        out_shape=tuple(outs),
        in_specs=[pl.BlockSpec(memory_space=pltpu.SMEM if a.size == 1 else space) for a in args]
        + [pl.BlockSpec(memory_space=pl.ANY)] * len(after),
        out_specs=tuple(pl.BlockSpec(memory_space=out_space) for _ in outs),
        scratch_shapes=list(scratch),
        input_output_aliases=aliases or {},
        compiler_params=pltpu.CompilerParams(vmem_limit_bytes=32 << 20),
        cost_estimate=pl.CostEstimate(flops=flops, bytes_accessed=moved, transcendentals=0),
    )(*held, *after)


def sds(shape, dtype):
    return jax.ShapeDtypeStruct(shape, dtype)


def swap(value, axis, mask):
    count = lax.axis_size(axis)
    return lax.ppermute(value, axis, [(s, s ^ mask) for s in range(count)])


def first_mask(core):
    return 1 + core


def cross(value, first):
    peers, shards = lax.axis_size("tm"), lax.axis_size("dp")
    pairs = []
    for t in range(peers):
        for d in range(shards):
            mask = first_mask(d % 2) if first else 3 - first_mask(d % 2)
            pairs.append((t * shards + d, (t ^ mask) * shards + d))
    return lax.ppermute(value, ("tm", "dp"), pairs)


def peer_block(turn):
    me = lax.axis_index("tm")
    if turn in (0, 3):
        return me ^ turn
    mask = first_mask(lax.axis_index("dp") % 2)
    return me ^ (mask if turn == 1 else 3 - mask)


def swaps(values, axis, step):
    got = []
    for m, value in enumerate(values):
        got.append(swap(value, axis, (m + 1) * step))
    return got


def low_half(shape):
    return lax.broadcasted_iota(jnp.int32, shape, len(shape) - 1) < LANES // 2


def half_turn(value):
    return pltpu.roll(value, LANES // 2, axis=1)


def column_shift(value, step, width):
    if step == 0:
        return value
    rows = value.shape[0]
    turned = pltpu.roll(value, (-step) % rows, axis=0)
    column = lax.broadcasted_iota(jnp.int32, value.shape, 0) % width
    edge = width - 1 if step > 0 else 0
    return jnp.where(column == edge, jnp.zeros_like(turned), turned)


def row_shift(value, step, width):
    if step == 0:
        return value
    blank = jnp.zeros((width, value.shape[1]), value.dtype)
    if step > 0:
        return jnp.concatenate([value[width:], blank], axis=0)
    return jnp.concatenate([blank, value[:-width]], axis=0)


def kept(length_ref, frame):
    return jnp.where(frame < length_ref[0], 1.0, 0.0).astype(F32)


def slice_body(peers, area, cot_hbm, clips_hbm, *refs):
    outs, own = refs[:peers], refs[peers]
    cot, picks, sems = refs[peers + 1 :]
    copies = []
    for tile in range(cot.shape[0]):
        lanes = pl.ds(tile * LANES, LANES)
        copies.append(pltpu.make_async_copy(cot_hbm.at[:, lanes], cot.at[tile], sems.at[tile]))
    own_copy = pltpu.make_async_copy(clips_hbm, own, sems.at[len(copies)])
    for copy in (*copies, own_copy):
        copy.start()
    low = low_half((area, LANES))
    halves = peers // len(copies)
    for tile, copy in enumerate(copies):
        copy.wait()
        first = cot[tile, :area, :].astype(F32)
        second = cot[tile, area:, :].astype(F32)
        picks[tile * halves] = jnp.where(low, first, half_turn(second))
        picks[tile * halves + 1] = jnp.where(low, half_turn(first), second)
    for turn, out in enumerate(outs):
        out[...] = picks[peer_block(turn)].astype(BF16)
    own_copy.wait()


def place_slice(area, width, length_ref, block, slice_ref, grads):
    low = low_half((area, LANES))
    start = pl.multiple_of(block * 2 * area, 2 * area)
    keep = jnp.where(low, kept(length_ref, 2 * block), kept(length_ref, 2 * block + 1))
    both = slice_ref[...].astype(F32) * keep
    taps = []
    for row_tap in range(3):
        for col_tap in range(3):
            moved = column_shift(both, 1 - col_tap, width)
            turned = half_turn(moved)
            taps.append([row_shift(v, 1 - row_tap, width) for v in (moved, turned)])
    taps.append([jnp.zeros_like(both)] * 2)
    for tile in range(5):
        (even, even_turned), (odd, odd_turned) = taps[2 * tile], taps[2 * tile + 1]
        for frame in range(2):
            left, right = (even, odd_turned) if frame == 0 else (even_turned, odd)
            grads[pl.ds(start + frame * area, area), tile * LANES : (tile + 1) * LANES] = (
                jnp.where(low, left, right).astype(BF16)
            )


def cut_body(start, source, out_ref):
    out_ref[...] = source[start : start + out_ref.shape[0], :]


def turn_frame(act_t, turn, frame, values):
    area = values.shape[0]
    at = (2 * turn + frame) * area
    act_t[:, at : at + area] = jax.nn.silu(values.astype(F32)).astype(BF16).T


def turn_block(area, act_t, turn, ref):
    for frame in range(2):
        turn_frame(act_t, turn, frame, ref[frame * area : (frame + 1) * area, :])


def own_body(area, width, length_ref, own, slice_ref, act_t, grads):
    turn_block(area, act_t, 0, own)
    grads[grads.shape[0] - 2 * area :, :] = jnp.zeros((2 * area, grads.shape[1]), BF16)
    place_slice(area, width, length_ref, lax.axis_index("tm"), slice_ref, grads)


def windows(area, grads, turn, time_tap):
    at = pl.multiple_of((2 * peer_block(turn) + 2 - time_tap) * area, area)
    return grads[pl.ds(at, 2 * area), :]


def near_body(area, width, length_ref, slice_a, near_a, near_b, *refs):
    grads, act_t = refs[2:]
    place_slice(area, width, length_ref, peer_block(1), slice_a, grads)
    turn_block(area, act_t, 1, near_a)
    turn_block(area, act_t, 2, near_b)


def products_body(area, width, length_ref, slice_b, slice_3, act_t, _, grads, *outs):
    for turn, ref in ((2, slice_b), (3, slice_3)):
        place_slice(area, width, length_ref, peer_block(turn), ref, grads)
    for time_tap, out in enumerate(outs):
        used = [windows(area, grads, turn, time_tap) for turn in range(3)]
        out[...] = jnp.dot(
            act_t[...], jnp.concatenate(used, axis=0), preferred_element_type=F32
        )


def sums_shape(parts, count):
    if count % 32 == 0:
        return (parts, 13 * count + count // 2, LANES)
    return (parts, count, 14 * LANES)


def put_tile(ref, part, tile, value):
    count = value.shape[0]
    if ref.shape[2] != LANES:
        ref[part, :, tile * LANES : (tile + 1) * LANES] = value
        return
    if tile == 13:
        low = low_half((count // 2, LANES))
        value = jnp.where(low, value[: count // 2], half_turn(value[count // 2 :]))
    ref[part, tile * count : tile * count + value.shape[0], :] = value


def get_tile(ref, part, tile, count):
    if ref.shape[2] != LANES:
        return ref[part, :, tile * LANES : (tile + 1) * LANES]
    if tile < 13:
        return ref[part, tile * count : (tile + 1) * count, :]
    value = ref[part, tile * count :, :]
    return jnp.concatenate([value, half_turn(value)], axis=0)


def rows_for(ref, parts, count, core):
    if count % 32 == 0:
        found = [
            ref[pl.ds(pl.multiple_of((2 * z + core) * count, count), count), :]
            for z in range(parts)
        ]
        return jnp.concatenate(found, axis=0)
    full = ref[...].astype(F32)
    groups = [full[at * count : (at + 1) * count] for at in range(2 * parts)]
    found = [jnp.where(core == 0, groups[2 * z], groups[2 * z + 1]) for z in range(parts)]
    return jnp.concatenate(found, axis=0).astype(ref.dtype)


def core_sums(count, area, core, grads, turned, products, out_ref):
    parts = out_ref.shape[0]
    acts = rows_for(turned, parts, count, core)
    sums = []
    for time_tap, ref in enumerate(products):
        sums.append(
            rows_for(ref, parts, count, core)
            + jnp.dot(acts, windows(area, grads, 3, time_tap), preferred_element_type=F32)
        )
    tiles = [s[:, tile * LANES : (tile + 1) * LANES] for s in sums for tile in range(4)]
    last = [s[:, 4 * LANES :] for s in sums]
    low = low_half(last[0].shape)
    tiles.append(jnp.where(low, last[0], half_turn(last[1])))
    tiles.append(last[2])
    for part in range(parts):
        for at, tile in enumerate(tiles):
            value = tile[part * count : (part + 1) * count]
            put_tile(out_ref, part, at, value.astype(out_ref.dtype))


def send_body(count, area, grads, first, second, *refs):
    products, (send_ref, turned) = refs[:3], refs[3:]
    values = jnp.concatenate([first[...], second[...]], axis=0).astype(F32)
    turned[...] = jax.nn.silu(values).astype(BF16).T
    other = 1 - lax.axis_index("dp") % 2
    core_sums(count, area, other, grads, turned, products, send_ref)


def keep_body(count, area, grads, turned, *refs):
    core_sums(count, area, lax.axis_index("dp") % 2, grads, turned, refs[:3], refs[3])


def sum_body(arrived, radix, step, *refs):
    keep_ref, in_refs = refs[0], refs[1 : 1 + arrived]
    total = keep_ref[...]
    for ref in in_refs:
        total = total + ref[...].astype(F32)
    if radix == 1:
        refs[1 + arrived][...] = total[0].astype(BF16)
        return
    out_refs, held = refs[1 + arrived : -1], refs[-1]
    held[...] = total
    digit = (lax.axis_index("dp") // 2) // step % radix
    for mask, out in enumerate(out_refs):
        out[...] = held[pl.ds((digit ^ mask) * step, step)].astype(out.dtype)


def sum_over_clips(keep, send, after):
    arrived = [swap(send, "dp", 1)]
    while True:
        parts, count, lanes = keep.shape
        radix = 1 if parts == 1 else (4 if parts % 4 == 0 else 2)
        assert parts % radix == 0 and radix & (radix - 1) == 0, "dp size"
        step = parts // radix
        if radix == 1:
            return call(
                functools.partial(sum_body, len(arrived), 1, 1),
                [pltpu.VMEM((count, lanes), BF16)],
                (keep, *arrived),
                after=after,
            )[0]
        outs = [pltpu.VMEM((step, count, lanes), F32)]
        outs += [pltpu.VMEM((step, count, lanes), BF16)] * (radix - 1)
        keep, *sends = call(
            functools.partial(sum_body, len(arrived), radix, step),
            outs,
            (keep, *arrived),
            scratch=[pltpu.VMEM((parts, count, lanes), F32)],
        )
        arrived = swaps(sends, "dp", 2 * step)


def place_body(peers, scale, *refs):
    pieces, out_hbm, held, placed, sems = refs[:peers], *refs[peers:]
    for turn, piece in enumerate(pieces):
        held[lax.axis_index("tm") ^ turn] = piece[...].astype(F32) * scale
    count = placed.shape[1]
    low = low_half((count, LANES))
    copies = []
    for time_tap in range(3):
        for tap in range(9):
            tile = 4 * time_tap + tap // 2 if tap < 8 else 12 + time_tap // 2
            half = tap % 2 if tap < 8 else time_tap % 2
            for pair in range(peers // 2):
                left = get_tile(held, 2 * pair, tile, count)
                right = get_tile(held, 2 * pair + 1, tile, count)
                if half == 0:
                    value = jnp.where(low, left, half_turn(right))
                else:
                    value = jnp.where(low, half_turn(left), right)
                placed[9 * time_tap + tap, :, pair * LANES : (pair + 1) * LANES] = value
        taps = pl.ds(9 * time_tap, 9)
        copies.append(pltpu.make_async_copy(placed.at[taps], out_hbm.at[taps], sems.at[time_tap]))
        copies[-1].start()
    for copy in copies:
        copy.wait()


def fill_padded(out_ref, frame, value, width, height, direction):
    wide = value.shape[1]
    blank = jnp.zeros((width, 3 * wide), BF16)
    out_ref[frame, :width, :] = blank
    out_ref[frame, (height + 1) * width :, :] = blank
    for tap in range(3):
        out_ref[frame, width : (height + 1) * width, tap * wide : (tap + 1) * wide] = column_shift(
            value, direction * (tap - 1), width
        ).astype(BF16)


def turn_taps(w_ref, out_ref, at):
    wide = w_ref.shape[2]
    for tap in range(3):
        rows = slice(tap * wide, (tap + 1) * wide)
        out_ref[at, rows, :] = w_ref[at, rows, :].T


def ahead_body(area, width, length_ref, own, near_a, near_b, first, second, w_ref, *refs):
    out_ref, token_ref, turned_ref, acts = refs
    token_ref[...] = jnp.zeros_like(token_ref)
    me = lax.axis_index("tm")
    height = area // width
    far = jnp.concatenate([first[...], second[...]], axis=0)
    for frame in range(2):
        rows = slice(frame * area, (frame + 1) * area)
        value = jnp.zeros((area, far.shape[1]), F32)
        for turn, block in ((1, near_a[rows, :]), (2, near_b[rows, :]), (3, far[rows])):
            value = jnp.where(peer_block(turn) == me - 1, block.astype(F32), value)
        fill_padded(acts, frame, jax.nn.silu(value), width, height, 1)
        value = own[rows, :].astype(F32)
        fill_padded(acts, 2 + frame, jax.nn.silu(value), width, height, 1)
    for frame in range(2):
        rows = slice(frame * area, (frame + 1) * area)
        total = jnp.zeros((area, out_ref.shape[1]), F32)
        for time_tap in range(3):
            for row_tap in range(3):
                window = acts[frame + time_tap, row_tap * width : row_tap * width + area, :]
                at = 3 * time_tap + row_tap
                total = total + jnp.dot(window, w_ref[at], preferred_element_type=F32)
                if frame == 0:
                    turn_taps(w_ref, turned_ref, at)
        out_ref[rows, :] = (total * kept(length_ref, 2 * me + frame)).astype(BF16)


def back_body(area, width, total_clips, length_ref, own, cot, later, wt_ref, gin_ref, grads):
    me = lax.axis_index("tm")
    height = area // width
    for frame in range(2):
        rows = slice(frame * area, (frame + 1) * area)
        for at, ref in ((frame, cot), (2 + frame, later)):
            value = ref[rows, :].astype(F32) * kept(length_ref, 2 * me + at)
            fill_padded(grads, at, value, width, height, -1)
    for frame in range(2):
        rows = slice(frame * area, (frame + 1) * area)
        total = jnp.zeros((area, gin_ref.shape[1]), F32)
        for time_tap in range(3):
            for row_tap in range(3):
                first = (2 - row_tap) * width
                window = grads[frame + 2 - time_tap, first : first + area, :]
                total = total + jnp.dot(
                    window, wt_ref[3 * time_tap + row_tap], preferred_element_type=F32
                )
        values = own[rows, :].astype(F32)
        sig = jax.nn.sigmoid(values)
        slope = sig * (1.0 + values * (1.0 - sig))
        keep = kept(length_ref, 2 * me + frame)
        gin_ref[rows, :] = (total * slope * (keep / total_clips)).astype(BF16)


def local(video_clips, cotangent, weight, lengths):
    clip_count, frame_count, height, width, channels = video_clips.shape
    peers, shards = lax.axis_size("tm"), lax.axis_size("dp")
    total_clips = clip_count * shards
    area = height * width
    assert clip_count == 1 and frame_count == 2, "block shape"
    assert 2 * channels == peers * LANES and peers == 4, "tm size"
    clips = video_clips.reshape(2 * area, channels)
    cot = cotangent.reshape(2 * area, channels)

    block = (2 * area, channels)
    near_a = cross(clips, True)
    near_b = cross(clips, False)
    *slices, own = call(
        functools.partial(slice_body, peers, area),
        [pltpu.VMEM((area, LANES), BF16)] * peers + [pltpu.VMEM(block, BF16)],
        (cot, clips),
        resident=False,
        scratch=[
            pltpu.VMEM((channels // LANES, 2 * area, LANES), BF16),
            pltpu.VMEM((peers, area, LANES), F32),
            pltpu.SemaphoreType.DMA((channels // LANES + 1,)),
        ],
    )
    slices[1] = cross(slices[1], True)
    slices[2] = cross(slices[2], False)
    slices[3] = swap(slices[3], "tm", 3)
    split = area
    relayed = [
        call(functools.partial(cut_body, start), [pltpu.VMEM((size, channels), BF16)], (near,))[0]
        for start, size, near in ((0, split, near_a), (split, 2 * area - split, near_b))
    ]
    first = cross(relayed[0], False)
    second = cross(relayed[1], True)
    later = lax.ppermute(cot, "tm", [(s, s - 1) for s in range(1, peers)])
    moved = pltpu.VMEM((2 * (peers + 1) * area, 5 * LANES), BF16)
    turned_acts = pltpu.VMEM((channels, 6 * area), BF16)
    act_t, grads = call(
        functools.partial(own_body, area, width), [turned_acts, moved], (lengths, own, slices[0])
    )
    parts = shards // 2
    count = channels // shards
    grads, act_t = call(
        functools.partial(near_body, area, width),
        [moved, turned_acts],
        (lengths, slices[1], near_a, near_b, grads, act_t),
        aliases={4: 0, 5: 1},
    )
    grads, *products = call(
        functools.partial(products_body, area, width),
        [moved] + [pltpu.VMEM((channels, 5 * LANES), F32)] * 3,
        (lengths, slices[2], slices[3], act_t, grads),
        aliases={4: 0},
        flops=2 * 27 * 2 * peers * area * channels * LANES // 2,
    )
    half = 27 * 2 * area * channels * LANES // 2
    send, last_turned = call(
        functools.partial(send_body, count, area),
        [pltpu.VMEM(sums_shape(parts, count), BF16), pltpu.VMEM((channels, 2 * area), BF16)],
        (grads, first, second, *products),
        flops=half,
    )
    (keep,) = call(
        functools.partial(keep_body, count, area),
        [pltpu.VMEM(sums_shape(parts, count), F32)],
        (grads, last_turned, *products),
        after=(send,),
        flops=half,
    )
    flat = weight.reshape(9, 3 * channels, channels)
    token = pltpu.VMEM((8, LANES), F32)
    padded = pltpu.VMEM((4, area + 2 * width, 3 * channels), BF16)
    flops = 2 * 27 * 2 * area * channels * channels
    conv_out, token_a, turned = call(
        functools.partial(ahead_body, area, width),
        [sds(block, BF16), token, pltpu.VMEM(flat.shape, BF16)],
        (lengths, own, near_a, near_b, first, second, flat),
        after=(keep,),
        scratch=[padded],
        flops=flops,
    )
    piece = sum_over_clips(keep, send, (token_a,))
    (input_grad,) = call(
        functools.partial(back_body, area, width, total_clips),
        [sds(block, BF16)],
        (lengths, own, cot, later, turned),
        after=(piece,),
        scratch=[padded],
        flops=flops,
    )
    pieces = [piece] + swaps([piece] * (peers - 1), "tm", 1)
    (placed,) = call(
        functools.partial(place_body, peers, 1.0 / total_clips),
        [sds((27, count, channels), F32)],
        pieces,
        scratch=[
            pltpu.VMEM((peers, *piece.shape), F32),
            pltpu.VMEM((27, count, channels), F32),
            pltpu.SemaphoreType.DMA((3,)),
        ],
        out_space=pl.ANY,
    )
    shape = video_clips.shape
    weight_grad = placed.reshape(3, 3, 3, count, channels)
    return conv_out.reshape(shape), input_grad.reshape(shape), weight_grad


def cuts(parts):
    found = []
    while parts > 1:
        if parts % 4 == 0:
            found.append(parts)
        parts //= 4 if parts % 4 == 0 else 2
    return found


def solution(mesh):
    in_specs = (P("dp", "tm", None, None, None), P("dp", "tm", None, None, None), P(), P("dp"))
    out_specs = (
        P("dp", "tm", None, None, None),
        P("dp", "tm", None, None, None),
        P(None, None, None, "dp", None),
    )

    program = jax.shard_map(local, mesh=mesh, in_specs=in_specs, out_specs=out_specs, check_vma=False)
    sizes = cuts(mesh.shape["dp"] // 2)
    assert sizes, "dp size"
    return program
```

```python
import functools

import jax
import jax.numpy as jnp
from jax import lax
from jax.experimental import pallas as pl
from jax.experimental.pallas import tpu as pltpu
from jax.sharding import PartitionSpec as P


F32 = jnp.float32
BF16 = jnp.bfloat16
LANES = 128


def call(
    body, outs, args, *, after=(), resident=True, scratch=(), flops=0, aliases=None,
    out_space=pltpu.VMEM,
):
    moved = sum(a.size * a.dtype.itemsize for a in args)
    space = pltpu.VMEM if resident else pltpu.HBM
    held = [a if a.size == 1 else pltpu.with_memory_space_constraint(a, space) for a in args]
    count = len(args)

    def with_after(*refs):
        body(*refs[:count], *refs[count + len(after) :])

    return pl.pallas_call(
        with_after,
        out_shape=tuple(outs),
        in_specs=[pl.BlockSpec(memory_space=pltpu.SMEM if a.size == 1 else space) for a in args]
        + [pl.BlockSpec(memory_space=pl.ANY)] * len(after),
        out_specs=tuple(pl.BlockSpec(memory_space=out_space) for _ in outs),
        scratch_shapes=list(scratch),
        input_output_aliases=aliases or {},
        compiler_params=pltpu.CompilerParams(vmem_limit_bytes=32 << 20),
        cost_estimate=pl.CostEstimate(flops=flops, bytes_accessed=moved, transcendentals=0),
    )(*held, *after)


def sds(shape, dtype):
    return jax.ShapeDtypeStruct(shape, dtype)


def swap(value, axis, mask):
    count = lax.axis_size(axis)
    return lax.ppermute(value, axis, [(s, s ^ mask) for s in range(count)])


def first_mask(core):
    return 1 + core


def cross(value, first):
    peers, shards = lax.axis_size("tm"), lax.axis_size("dp")
    pairs = []
    for t in range(peers):
        for d in range(shards):
            mask = first_mask(d % 2) if first else 3 - first_mask(d % 2)
            pairs.append((t * shards + d, (t ^ mask) * shards + d))
    return lax.ppermute(value, ("tm", "dp"), pairs)


def peer_block(turn):
    me = lax.axis_index("tm")
    if turn in (0, 3):
        return me ^ turn
    mask = first_mask(lax.axis_index("dp") % 2)
    return me ^ (mask if turn == 1 else 3 - mask)


def swaps(values, axis, step):
    got = []
    for m, value in enumerate(values):
        got.append(swap(value, axis, (m + 1) * step))
    return got


def low_half(shape):
    return lax.broadcasted_iota(jnp.int32, shape, len(shape) - 1) < LANES // 2


def half_turn(value):
    return pltpu.roll(value, LANES // 2, axis=1)


def column_shift(value, step, width):
    if step == 0:
        return value
    rows = value.shape[0]
    turned = pltpu.roll(value, (-step) % rows, axis=0)
    column = lax.broadcasted_iota(jnp.int32, value.shape, 0) % width
    edge = width - 1 if step > 0 else 0
    return jnp.where(column == edge, jnp.zeros_like(turned), turned)


def row_shift(value, step, width):
    if step == 0:
        return value
    blank = jnp.zeros((width, value.shape[1]), value.dtype)
    if step > 0:
        return jnp.concatenate([value[width:], blank], axis=0)
    return jnp.concatenate([blank, value[:-width]], axis=0)


def kept(length_ref, frame):
    return jnp.where(frame < length_ref[0], 1.0, 0.0).astype(F32)


def slice_body(peers, area, cot_hbm, clips_hbm, *refs):
    outs, own = refs[:peers], refs[peers]
    cot, picks, sems = refs[peers + 1 :]
    copies = []
    for tile in range(cot.shape[0]):
        lanes = pl.ds(tile * LANES, LANES)
        copies.append(pltpu.make_async_copy(cot_hbm.at[:, lanes], cot.at[tile], sems.at[tile]))
    own_copy = pltpu.make_async_copy(clips_hbm, own, sems.at[len(copies)])
    for copy in (*copies, own_copy):
        copy.start()
    low = low_half((area, LANES))
    halves = peers // len(copies)
    for tile, copy in enumerate(copies):
        copy.wait()
        first = cot[tile, :area, :].astype(F32)
        second = cot[tile, area:, :].astype(F32)
        picks[tile * halves] = jnp.where(low, first, half_turn(second))
        picks[tile * halves + 1] = jnp.where(low, half_turn(first), second)
    for turn, out in enumerate(outs):
        out[...] = picks[peer_block(turn)].astype(BF16)
    own_copy.wait()


def place_slice(area, width, length_ref, block, slice_ref, grads):
    low = low_half((area, LANES))
    start = pl.multiple_of(block * 2 * area, 2 * area)
    keep = jnp.where(low, kept(length_ref, 2 * block), kept(length_ref, 2 * block + 1))
    both = slice_ref[...].astype(F32) * keep
    taps = []
    for row_tap in range(3):
        for col_tap in range(3):
            moved = column_shift(both, 1 - col_tap, width)
            turned = half_turn(moved)
            taps.append([row_shift(v, 1 - row_tap, width) for v in (moved, turned)])
    taps.append([jnp.zeros_like(both)] * 2)
    for tile in range(5):
        (even, even_turned), (odd, odd_turned) = taps[2 * tile], taps[2 * tile + 1]
        for frame in range(2):
            left, right = (even, odd_turned) if frame == 0 else (even_turned, odd)
            grads[pl.ds(start + frame * area, area), tile * LANES : (tile + 1) * LANES] = (
                jnp.where(low, left, right).astype(BF16)
            )


def cut_body(start, source, out_ref):
    out_ref[...] = source[start : start + out_ref.shape[0], :]


def turn_frame(act_t, turn, frame, values):
    area = values.shape[0]
    at = (2 * turn + frame) * area
    act_t[:, at : at + area] = jax.nn.silu(values.astype(F32)).astype(BF16).T


def turn_block(area, act_t, turn, ref):
    for frame in range(2):
        turn_frame(act_t, turn, frame, ref[frame * area : (frame + 1) * area, :])


def own_body(area, width, length_ref, own, slice_ref, act_t, grads):
    turn_block(area, act_t, 0, own)
    grads[grads.shape[0] - 2 * area :, :] = jnp.zeros((2 * area, grads.shape[1]), BF16)
    place_slice(area, width, length_ref, lax.axis_index("tm"), slice_ref, grads)


def windows(area, grads, turn, time_tap):
    at = pl.multiple_of((2 * peer_block(turn) + 2 - time_tap) * area, area)
    return grads[pl.ds(at, 2 * area), :]


def near_body(area, width, length_ref, slice_a, near_a, near_b, *refs):
    grads, act_t = refs[2:]
    place_slice(area, width, length_ref, peer_block(1), slice_a, grads)
    turn_block(area, act_t, 1, near_a)
    turn_block(area, act_t, 2, near_b)


def products_body(area, width, length_ref, slice_b, slice_3, act_t, _, grads, *outs):
    for turn, ref in ((2, slice_b), (3, slice_3)):
        place_slice(area, width, length_ref, peer_block(turn), ref, grads)
    for time_tap, out in enumerate(outs):
        used = [windows(area, grads, turn, time_tap) for turn in range(3)]
        out[...] = jnp.dot(
            act_t[...], jnp.concatenate(used, axis=0), preferred_element_type=F32
        )


def sums_shape(parts, count):
    if count % 32 == 0:
        return (parts, 13 * count + count // 2, LANES)
    return (parts, count, 14 * LANES)


def put_tile(ref, part, tile, value):
    count = value.shape[0]
    if ref.shape[2] != LANES:
        ref[part, :, tile * LANES : (tile + 1) * LANES] = value
        return
    if tile == 13:
        low = low_half((count // 2, LANES))
        value = jnp.where(low, value[: count // 2], half_turn(value[count // 2 :]))
    ref[part, tile * count : tile * count + value.shape[0], :] = value


def get_tile(ref, part, tile, count):
    if ref.shape[2] != LANES:
        return ref[part, :, tile * LANES : (tile + 1) * LANES]
    if tile < 13:
        return ref[part, tile * count : (tile + 1) * count, :]
    value = ref[part, tile * count :, :].astype(F32)
    return jnp.concatenate([value, half_turn(value)], axis=0)


def rows_for(ref, parts, count, core):
    if count % 32 == 0:
        found = [
            ref[pl.ds(pl.multiple_of((2 * z + core) * count, count), count), :]
            for z in range(parts)
        ]
        return jnp.concatenate(found, axis=0)
    full = ref[...].astype(F32)
    groups = [full[at * count : (at + 1) * count] for at in range(2 * parts)]
    found = [jnp.where(core == 0, groups[2 * z], groups[2 * z + 1]) for z in range(parts)]
    return jnp.concatenate(found, axis=0).astype(ref.dtype)


def core_sums(count, area, core, grads, turned, products, out_ref):
    parts = out_ref.shape[0]
    acts = rows_for(turned, parts, count, core)
    sums = []
    for time_tap, ref in enumerate(products):
        sums.append(
            rows_for(ref, parts, count, core)
            + jnp.dot(acts, windows(area, grads, 3, time_tap), preferred_element_type=F32)
        )
    tiles = [s[:, tile * LANES : (tile + 1) * LANES] for s in sums for tile in range(4)]
    last = [s[:, 4 * LANES :] for s in sums]
    low = low_half(last[0].shape)
    tiles.append(jnp.where(low, last[0], half_turn(last[1])))
    tiles.append(last[2])
    for part in range(parts):
        for at, tile in enumerate(tiles):
            value = tile[part * count : (part + 1) * count]
            put_tile(out_ref, part, at, value.astype(out_ref.dtype))


def first_rows_body(first, turned):
    rows = first.shape[0]
    turned[:, :rows] = jax.nn.silu(first[...].astype(F32)).astype(BF16).T


def send_body(count, area, grads, second, held, *refs):
    products, (send_ref, turned) = refs[:3], refs[3:]
    rows = second.shape[0]
    turned[:, 2 * area - rows :] = jax.nn.silu(second[...].astype(F32)).astype(BF16).T
    other = 1 - lax.axis_index("dp") % 2
    core_sums(count, area, other, grads, turned, products, send_ref)


def keep_body(count, area, grads, turned, *refs):
    core_sums(count, area, lax.axis_index("dp") % 2, grads, turned, refs[:3], refs[3])


def sum_body(arrived, radix, step, *refs):
    terms, out_refs = refs[: 1 + arrived], refs[1 + arrived :]

    def total(part):
        return sum((ref[part].astype(F32) for ref in terms[1:]), terms[0][part])

    if radix == 1:
        out_refs[0][...] = total(0).astype(BF16)
        return
    digit = (lax.axis_index("dp") // 2) // step % radix
    for mask, out in enumerate(out_refs):
        out[...] = total(pl.ds((digit ^ mask) * step, step)).astype(out.dtype)


def sum_over_clips(keep, send, after):
    arrived = [swap(send, "dp", 1)]
    while True:
        parts, count, lanes = keep.shape
        radix = 1 if parts == 1 else (4 if parts % 4 == 0 else 2)
        assert parts % radix == 0 and radix & (radix - 1) == 0, "dp size"
        step = parts // radix
        if radix == 1:
            return call(
                functools.partial(sum_body, len(arrived), 1, 1),
                [pltpu.VMEM((count, lanes), BF16)],
                (keep, *arrived),
                after=after,
            )[0]
        outs = [pltpu.VMEM((step, count, lanes), F32)]
        outs += [pltpu.VMEM((step, count, lanes), BF16)] * (radix - 1)
        keep, *sends = call(
            functools.partial(sum_body, len(arrived), radix, step), outs, (keep, *arrived)
        )
        arrived = swaps(sends, "dp", 2 * step)


def place_body(peers, scale, *refs):
    pieces, out_hbm, held, placed, sems = refs[:peers], *refs[peers:]
    for mask, piece in enumerate(pieces):
        held[lax.axis_index("tm") ^ mask] = piece[...]
    count = placed.shape[1]
    low = low_half((count, LANES))
    copies = []
    for tap in range(27):
        time_tap, at = tap // 9, tap % 9
        tile = 4 * time_tap + at // 2 if at < 8 else 12 + time_tap // 2
        half = at % 2 if at < 8 else time_tap % 2
        for pair in range(peers // 2):
            left = get_tile(held, 2 * pair, tile, count).astype(F32)
            right = get_tile(held, 2 * pair + 1, tile, count).astype(F32)
            if half == 0:
                value = jnp.where(low, left, half_turn(right))
            else:
                value = jnp.where(low, half_turn(left), right)
            placed[tap, :, pair * LANES : (pair + 1) * LANES] = value * scale
        if tap % 3 == 2:
            taps = pl.ds(tap - 2, 3)
            copies.append(
                pltpu.make_async_copy(placed.at[taps], out_hbm.at[taps], sems.at[tap // 3])
            )
            copies[-1].start()
    for copy in copies:
        copy.wait()


def fill_padded(out_ref, frame, value, width, height, direction):
    wide = value.shape[1]
    blank = jnp.zeros((width, 3 * wide), BF16)
    out_ref[frame, :width, :] = blank
    out_ref[frame, (height + 1) * width :, :] = blank
    for tap in range(3):
        out_ref[frame, width : (height + 1) * width, tap * wide : (tap + 1) * wide] = column_shift(
            value, direction * (tap - 1), width
        ).astype(BF16)


def turn_taps(w_ref, out_ref, at):
    wide = w_ref.shape[2]
    for tap in range(3):
        rows = slice(tap * wide, (tap + 1) * wide)
        out_ref[at, rows, :] = w_ref[at, rows, :].T


def ahead_body(area, width, length_ref, own, near_a, near_b, first, second, w_ref, *refs):
    out_ref, token_ref, turned_ref, acts = refs
    token_ref[...] = jnp.zeros_like(token_ref)
    me = lax.axis_index("tm")
    height = area // width
    far = jnp.concatenate([first[...], second[...]], axis=0)
    for frame in range(2):
        rows = slice(frame * area, (frame + 1) * area)
        value = jnp.zeros((area, far.shape[1]), F32)
        for turn, block in ((1, near_a[rows, :]), (2, near_b[rows, :]), (3, far[rows])):
            value = jnp.where(peer_block(turn) == me - 1, block.astype(F32), value)
        fill_padded(acts, frame, jax.nn.silu(value), width, height, 1)
        value = own[rows, :].astype(F32)
        fill_padded(acts, 2 + frame, jax.nn.silu(value), width, height, 1)
    for frame in range(2):
        rows = slice(frame * area, (frame + 1) * area)
        total = jnp.zeros((area, out_ref.shape[1]), F32)
        for time_tap in range(3):
            for row_tap in range(3):
                window = acts[frame + time_tap, row_tap * width : row_tap * width + area, :]
                at = 3 * time_tap + row_tap
                total = total + jnp.dot(window, w_ref[at], preferred_element_type=F32)
                if frame == 0:
                    turn_taps(w_ref, turned_ref, at)
        out_ref[rows, :] = (total * kept(length_ref, 2 * me + frame)).astype(BF16)


def back_body(area, width, total_clips, length_ref, own, cot, later, wt_ref, gin_ref, grads):
    me = lax.axis_index("tm")
    height = area // width
    for frame in range(2):
        rows = slice(frame * area, (frame + 1) * area)
        for at, ref in ((frame, cot), (2 + frame, later)):
            value = ref[rows, :].astype(F32) * kept(length_ref, 2 * me + at)
            fill_padded(grads, at, value, width, height, -1)
    for frame in range(2):
        rows = slice(frame * area, (frame + 1) * area)
        total = jnp.zeros((area, gin_ref.shape[1]), F32)
        for time_tap in range(3):
            for row_tap in range(3):
                first = (2 - row_tap) * width
                window = grads[frame + 2 - time_tap, first : first + area, :]
                total = total + jnp.dot(
                    window, wt_ref[3 * time_tap + row_tap], preferred_element_type=F32
                )
        values = own[rows, :].astype(F32)
        sig = jax.nn.sigmoid(values)
        slope = sig * (1.0 + values * (1.0 - sig))
        keep = kept(length_ref, 2 * me + frame)
        gin_ref[rows, :] = (total * slope * (keep / total_clips)).astype(BF16)


def local(video_clips, cotangent, weight, lengths):
    clip_count, frame_count, height, width, channels = video_clips.shape
    peers, shards = lax.axis_size("tm"), lax.axis_size("dp")
    total_clips = clip_count * shards
    area = height * width
    assert clip_count == 1 and frame_count == 2, "block shape"
    assert 2 * channels == peers * LANES and peers == 4, "tm size"
    clips = video_clips.reshape(2 * area, channels)
    cot = cotangent.reshape(2 * area, channels)

    block = (2 * area, channels)
    near_a = cross(clips, True)
    near_b = cross(clips, False)
    *slices, own = call(
        functools.partial(slice_body, peers, area),
        [pltpu.VMEM((area, LANES), BF16)] * peers + [pltpu.VMEM(block, BF16)],
        (cot, clips),
        resident=False,
        scratch=[
            pltpu.VMEM((channels // LANES, 2 * area, LANES), BF16),
            pltpu.VMEM((peers, area, LANES), F32),
            pltpu.SemaphoreType.DMA((channels // LANES + 1,)),
        ],
    )
    slices[1] = cross(slices[1], True)
    slices[2] = cross(slices[2], False)
    slices[3] = swap(slices[3], "tm", 3)
    split = area
    relayed = [
        call(functools.partial(cut_body, start), [pltpu.VMEM((size, channels), BF16)], (near,))[0]
        for start, size, near in ((0, split, near_a), (split, 2 * area - split, near_b))
    ]
    first = cross(relayed[0], False)
    second = cross(relayed[1], True)
    later = lax.ppermute(cot, "tm", [(s, s - 1) for s in range(1, peers)])
    moved = pltpu.VMEM((2 * (peers + 1) * area, 5 * LANES), BF16)
    turned_acts = pltpu.VMEM((channels, 6 * area), BF16)
    act_t, grads = call(
        functools.partial(own_body, area, width), [turned_acts, moved], (lengths, own, slices[0])
    )
    parts = shards // 2
    count = channels // shards
    grads, act_t = call(
        functools.partial(near_body, area, width),
        [moved, turned_acts],
        (lengths, slices[1], near_a, near_b, grads, act_t),
        aliases={4: 0, 5: 1},
    )
    grads, *products = call(
        functools.partial(products_body, area, width),
        [moved] + [pltpu.VMEM((channels, 5 * LANES), F32)] * 3,
        (lengths, slices[2], slices[3], act_t, grads),
        aliases={4: 0},
        flops=2 * 27 * 2 * peers * area * channels * LANES // 2,
    )
    half = 27 * 2 * area * channels * LANES // 2
    last = pltpu.VMEM((channels, 2 * area), BF16)
    (last_turned,) = call(first_rows_body, [last], (first,))
    send, last_turned = call(
        functools.partial(send_body, count, area),
        [pltpu.VMEM(sums_shape(parts, count), BF16), last],
        (grads, second, last_turned, *products),
        aliases={2: 1},
        flops=half,
    )
    (keep,) = call(
        functools.partial(keep_body, count, area),
        [pltpu.VMEM(sums_shape(parts, count), F32)],
        (grads, last_turned, *products),
        after=(send,),
        flops=half,
    )
    flat = weight.reshape(9, 3 * channels, channels)
    token = pltpu.VMEM((8, LANES), F32)
    padded = pltpu.VMEM((4, area + 2 * width, 3 * channels), BF16)
    flops = 2 * 27 * 2 * area * channels * channels
    conv_out, token_a, turned = call(
        functools.partial(ahead_body, area, width),
        [sds(block, BF16), token, pltpu.VMEM(flat.shape, BF16)],
        (lengths, own, near_a, near_b, first, second, flat),
        after=(keep,),
        scratch=[padded],
        flops=flops,
    )
    piece = sum_over_clips(keep, send, (token_a,))
    (input_grad,) = call(
        functools.partial(back_body, area, width, total_clips),
        [sds(block, BF16)],
        (lengths, own, cot, later, turned),
        after=(piece,),
        scratch=[padded],
        flops=flops,
    )
    pieces = [piece] + swaps([piece] * (peers - 1), "tm", 1)
    (placed,) = call(
        functools.partial(place_body, peers, 1.0 / total_clips),
        [sds((27, count, channels), F32)],
        pieces,
        scratch=[
            pltpu.VMEM((peers, *piece.shape), BF16),
            pltpu.VMEM((27, count, channels), F32),
            pltpu.SemaphoreType.DMA((9,)),
        ],
        out_space=pl.ANY,
    )
    shape = video_clips.shape
    weight_grad = placed.reshape(3, 3, 3, count, channels)
    return conv_out.reshape(shape), input_grad.reshape(shape), weight_grad


def cuts(parts):
    found = []
    while parts > 1:
        if parts % 4 == 0:
            found.append(parts)
        parts //= 4 if parts % 4 == 0 else 2
    return found


def solution(mesh):
    in_specs = (P("dp", "tm", None, None, None), P("dp", "tm", None, None, None), P(), P("dp"))
    out_specs = (
        P("dp", "tm", None, None, None),
        P("dp", "tm", None, None, None),
        P(None, None, None, "dp", None),
    )

    program = jax.shard_map(local, mesh=mesh, in_specs=in_specs, out_specs=out_specs, check_vma=False)
    sizes = cuts(mesh.shape["dp"] // 2)
    assert sizes, "dp size"
    return program
```

```python
import functools

import jax
import jax.numpy as jnp
from jax import lax
from jax.experimental import pallas as pl
from jax.experimental.pallas import tpu as pltpu
from jax.sharding import PartitionSpec as P


F32 = jnp.float32
BF16 = jnp.bfloat16
LANES = 128


def call(
    body, outs, args, *, after=(), resident=True, scratch=(), flops=0, aliases=None,
    out_space=pltpu.VMEM,
):
    moved = sum(a.size * a.dtype.itemsize for a in args)
    space = pltpu.VMEM if resident else pltpu.HBM
    held = [a if a.size == 1 else pltpu.with_memory_space_constraint(a, space) for a in args]
    count = len(args)

    def with_after(*refs):
        body(*refs[:count], *refs[count + len(after) :])

    return pl.pallas_call(
        with_after,
        out_shape=tuple(outs),
        in_specs=[pl.BlockSpec(memory_space=pltpu.SMEM if a.size == 1 else space) for a in args]
        + [pl.BlockSpec(memory_space=pl.ANY)] * len(after),
        out_specs=tuple(pl.BlockSpec(memory_space=out_space) for _ in outs),
        scratch_shapes=list(scratch),
        input_output_aliases=aliases or {},
        compiler_params=pltpu.CompilerParams(vmem_limit_bytes=32 << 20),
        cost_estimate=pl.CostEstimate(flops=flops, bytes_accessed=moved, transcendentals=0),
    )(*held, *after)


def sds(shape, dtype):
    return jax.ShapeDtypeStruct(shape, dtype)


def swap(value, axis, mask):
    count = lax.axis_size(axis)
    return lax.ppermute(value, axis, [(s, s ^ mask) for s in range(count)])


def first_mask(core):
    return 1 + core


def cross(value, first):
    peers, shards = lax.axis_size("tm"), lax.axis_size("dp")
    pairs = []
    for t in range(peers):
        for d in range(shards):
            mask = first_mask(d % 2) if first else 3 - first_mask(d % 2)
            pairs.append((t * shards + d, (t ^ mask) * shards + d))
    return lax.ppermute(value, ("tm", "dp"), pairs)


def peer_block(turn):
    me = lax.axis_index("tm")
    if turn in (0, 3):
        return me ^ turn
    mask = first_mask(lax.axis_index("dp") % 2)
    return me ^ (mask if turn == 1 else 3 - mask)


def swaps(values, axis, step):
    got = []
    for m, value in enumerate(values):
        got.append(swap(value, axis, (m + 1) * step))
    return got


def low_half(shape):
    return lax.broadcasted_iota(jnp.int32, shape, len(shape) - 1) < LANES // 2


def half_turn(value):
    return pltpu.roll(value, LANES // 2, axis=1)


def column_shift(value, step, width):
    if step == 0:
        return value
    rows = value.shape[0]
    turned = pltpu.roll(value, (-step) % rows, axis=0)
    column = lax.broadcasted_iota(jnp.int32, value.shape, 0) % width
    edge = width - 1 if step > 0 else 0
    return jnp.where(column == edge, jnp.zeros_like(turned), turned)


def row_shift(value, step, width):
    if step == 0:
        return value
    blank = jnp.zeros((width, value.shape[1]), value.dtype)
    if step > 0:
        return jnp.concatenate([value[width:], blank], axis=0)
    return jnp.concatenate([blank, value[:-width]], axis=0)


def kept(length_ref, frame):
    return jnp.where(frame < length_ref[0], 1.0, 0.0).astype(F32)


def slice_body(peers, area, cot_hbm, clips_hbm, *refs):
    outs, own = refs[:peers], refs[peers]
    cot, picks, sems = refs[peers + 1 :]
    copies = []
    for tile in range(cot.shape[0]):
        lanes = pl.ds(tile * LANES, LANES)
        copies.append(pltpu.make_async_copy(cot_hbm.at[:, lanes], cot.at[tile], sems.at[tile]))
    own_copy = pltpu.make_async_copy(clips_hbm, own, sems.at[len(copies)])
    for copy in (*copies, own_copy):
        copy.start()
    low = low_half((area, LANES))
    halves = peers // len(copies)
    for tile, copy in enumerate(copies):
        copy.wait()
        first = cot[tile, :area, :].astype(F32)
        second = cot[tile, area:, :].astype(F32)
        picks[tile * halves] = jnp.where(low, first, half_turn(second))
        picks[tile * halves + 1] = jnp.where(low, half_turn(first), second)
    for turn, out in enumerate(outs):
        out[...] = picks[peer_block(turn)].astype(BF16)
    own_copy.wait()


def place_slice(area, width, length_ref, block, slice_ref, grads):
    low = low_half((area, LANES))
    start = pl.multiple_of(block * 2 * area, 2 * area)
    keep = jnp.where(low, kept(length_ref, 2 * block), kept(length_ref, 2 * block + 1))
    both = slice_ref[...].astype(F32) * keep
    taps = []
    for row_tap in range(3):
        for col_tap in range(3):
            moved = column_shift(both, 1 - col_tap, width)
            turned = half_turn(moved)
            taps.append([row_shift(v, 1 - row_tap, width) for v in (moved, turned)])
    taps.append([jnp.zeros_like(both)] * 2)
    for tile in range(5):
        (even, even_turned), (odd, odd_turned) = taps[2 * tile], taps[2 * tile + 1]
        for frame in range(2):
            left, right = (even, odd_turned) if frame == 0 else (even_turned, odd)
            grads[pl.ds(start + frame * area, area), tile * LANES : (tile + 1) * LANES] = (
                jnp.where(low, left, right).astype(BF16)
            )


def cut_body(start, source, out_ref):
    out_ref[...] = source[start : start + out_ref.shape[0], :]


def turn_frame(act_t, turn, frame, values):
    area = values.shape[0]
    at = (2 * turn + frame) * area
    act_t[:, at : at + area] = jax.nn.silu(values.astype(F32)).astype(BF16).T


def turn_block(area, act_t, turn, ref):
    for frame in range(2):
        turn_frame(act_t, turn, frame, ref[frame * area : (frame + 1) * area, :])


def own_body(area, width, length_ref, own, slice_ref, act_t, grads):
    turn_block(area, act_t, 0, own)
    grads[grads.shape[0] - 2 * area :, :] = jnp.zeros((2 * area, grads.shape[1]), BF16)
    place_slice(area, width, length_ref, lax.axis_index("tm"), slice_ref, grads)


def windows(area, grads, turn, time_tap):
    at = pl.multiple_of((2 * peer_block(turn) + 2 - time_tap) * area, area)
    return grads[pl.ds(at, 2 * area), :]


def near_body(area, width, length_ref, slice_a, near_a, near_b, *refs):
    grads, act_t = refs[2:]
    place_slice(area, width, length_ref, peer_block(1), slice_a, grads)
    turn_block(area, act_t, 1, near_a)
    turn_block(area, act_t, 2, near_b)


def products_body(area, width, length_ref, slice_b, slice_3, act_t, _, grads, *outs):
    for turn, ref in ((2, slice_b), (3, slice_3)):
        place_slice(area, width, length_ref, peer_block(turn), ref, grads)
    for time_tap, out in enumerate(outs):
        used = [windows(area, grads, turn, time_tap) for turn in range(3)]
        out[...] = jnp.dot(
            act_t[...], jnp.concatenate(used, axis=0), preferred_element_type=F32
        )


def sums_shape(parts, count):
    if count % 32 == 0:
        return (parts, 13 * count + count // 2, LANES)
    return (parts, count, 14 * LANES)


def put_tile(ref, part, tile, value):
    count = value.shape[0]
    if ref.shape[2] != LANES:
        ref[part, :, tile * LANES : (tile + 1) * LANES] = value
        return
    if tile == 13:
        low = low_half((count // 2, LANES))
        value = jnp.where(low, value[: count // 2], half_turn(value[count // 2 :]))
    ref[part, tile * count : tile * count + value.shape[0], :] = value


def get_tile(ref, part, tile, count):
    if ref.shape[2] != LANES:
        return ref[part, :, tile * LANES : (tile + 1) * LANES]
    if tile < 13:
        return ref[part, tile * count : (tile + 1) * count, :]
    value = ref[part, tile * count :, :].astype(F32)
    return jnp.concatenate([value, half_turn(value)], axis=0)


def rows_for(ref, parts, count, core):
    if count % 32 == 0:
        found = [
            ref[pl.ds(pl.multiple_of((2 * z + core) * count, count), count), :]
            for z in range(parts)
        ]
        return jnp.concatenate(found, axis=0)
    full = ref[...].astype(F32)
    groups = [full[at * count : (at + 1) * count] for at in range(2 * parts)]
    found = [jnp.where(core == 0, groups[2 * z], groups[2 * z + 1]) for z in range(parts)]
    return jnp.concatenate(found, axis=0).astype(ref.dtype)


def core_sums(count, area, core, grads, turned, products, out_ref):
    parts = out_ref.shape[0]
    acts = rows_for(turned, parts, count, core)
    sums = []
    for time_tap, ref in enumerate(products):
        sums.append(
            rows_for(ref, parts, count, core)
            + jnp.dot(acts, windows(area, grads, 3, time_tap), preferred_element_type=F32)
        )
    tiles = [s[:, tile * LANES : (tile + 1) * LANES] for s in sums for tile in range(4)]
    last = [s[:, 4 * LANES :] for s in sums]
    low = low_half(last[0].shape)
    tiles.append(jnp.where(low, last[0], half_turn(last[1])))
    tiles.append(last[2])
    for part in range(parts):
        for at, tile in enumerate(tiles):
            value = tile[part * count : (part + 1) * count]
            put_tile(out_ref, part, at, value.astype(out_ref.dtype))


def send_body(count, area, grads, first, second, *refs):
    products, (send_ref, turned) = refs[:3], refs[3:]
    values = jnp.concatenate([first[...], second[...]], axis=0).astype(F32)
    turned[...] = jax.nn.silu(values).astype(BF16).T
    other = 1 - lax.axis_index("dp") % 2
    core_sums(count, area, other, grads, turned, products, send_ref)


def keep_body(count, area, grads, turned, *refs):
    core_sums(count, area, lax.axis_index("dp") % 2, grads, turned, refs[:3], refs[3])


def sum_body(arrived, radix, step, *refs):
    keep_ref, in_refs = refs[0], refs[1 : 1 + arrived]
    total = keep_ref[...]
    for ref in in_refs:
        total = total + ref[...].astype(F32)
    if radix == 1:
        refs[1 + arrived][...] = total[0].astype(BF16)
        return
    out_refs, held = refs[1 + arrived : -1], refs[-1]
    held[...] = total
    digit = (lax.axis_index("dp") // 2) // step % radix
    for mask, out in enumerate(out_refs):
        out[...] = held[pl.ds((digit ^ mask) * step, step)].astype(out.dtype)


def sum_over_clips(keep, send, after):
    arrived = [swap(send, "dp", 1)]
    while True:
        parts, count, lanes = keep.shape
        radix = 1 if parts == 1 else (4 if parts % 4 == 0 else 2)
        assert parts % radix == 0 and radix & (radix - 1) == 0, "dp size"
        step = parts // radix
        if radix == 1:
            return call(
                functools.partial(sum_body, len(arrived), 1, 1),
                [pltpu.VMEM((count, lanes), BF16)],
                (keep, *arrived),
                after=after,
            )[0]
        outs = [pltpu.VMEM((step, count, lanes), F32)]
        outs += [pltpu.VMEM((step, count, lanes), BF16)] * (radix - 1)
        keep, *sends = call(
            functools.partial(sum_body, len(arrived), radix, step),
            outs,
            (keep, *arrived),
            scratch=[pltpu.VMEM((parts, count, lanes), F32)],
        )
        arrived = swaps(sends, "dp", 2 * step)


def place_body(peers, scale, *refs):
    pieces, out_hbm, held, placed, sems = refs[:peers], *refs[peers:]
    for mask, piece in enumerate(pieces):
        held[lax.axis_index("tm") ^ mask] = piece[...]
    count = placed.shape[1]
    low = low_half((count, LANES))
    copies = []
    for tap in range(27):
        time_tap, at = tap // 9, tap % 9
        tile = 4 * time_tap + at // 2 if at < 8 else 12 + time_tap // 2
        half = at % 2 if at < 8 else time_tap % 2
        for pair in range(peers // 2):
            left = get_tile(held, 2 * pair, tile, count).astype(F32)
            right = get_tile(held, 2 * pair + 1, tile, count).astype(F32)
            if half == 0:
                value = jnp.where(low, left, half_turn(right))
            else:
                value = jnp.where(low, half_turn(left), right)
            placed[tap, :, pair * LANES : (pair + 1) * LANES] = value * scale
        if tap % 3 == 2:
            taps = pl.ds(tap - 2, 3)
            copies.append(
                pltpu.make_async_copy(placed.at[taps], out_hbm.at[taps], sems.at[tap // 3])
            )
            copies[-1].start()
    for copy in copies:
        copy.wait()


def fill_padded(out_ref, frame, value, width, height, direction):
    wide = value.shape[1]
    blank = jnp.zeros((width, 3 * wide), BF16)
    out_ref[frame, :width, :] = blank
    out_ref[frame, (height + 1) * width :, :] = blank
    for tap in range(3):
        out_ref[frame, width : (height + 1) * width, tap * wide : (tap + 1) * wide] = column_shift(
            value, direction * (tap - 1), width
        ).astype(BF16)


def turn_taps(w_ref, out_ref, at):
    wide = w_ref.shape[2]
    for tap in range(3):
        rows = slice(tap * wide, (tap + 1) * wide)
        out_ref[at, rows, :] = w_ref[at, rows, :].T


def ahead_body(area, width, length_ref, own, near_a, near_b, first, second, w_ref, *refs):
    out_ref, token_ref, turned_ref, acts = refs
    token_ref[...] = jnp.zeros_like(token_ref)
    me = lax.axis_index("tm")
    height = area // width
    far = jnp.concatenate([first[...], second[...]], axis=0)
    for frame in range(2):
        rows = slice(frame * area, (frame + 1) * area)
        value = jnp.zeros((area, far.shape[1]), F32)
        for turn, block in ((1, near_a[rows, :]), (2, near_b[rows, :]), (3, far[rows])):
            value = jnp.where(peer_block(turn) == me - 1, block.astype(F32), value)
        fill_padded(acts, frame, jax.nn.silu(value), width, height, 1)
        value = own[rows, :].astype(F32)
        fill_padded(acts, 2 + frame, jax.nn.silu(value), width, height, 1)
    for frame in range(2):
        rows = slice(frame * area, (frame + 1) * area)
        total = jnp.zeros((area, out_ref.shape[1]), F32)
        for time_tap in range(3):
            for row_tap in range(3):
                window = acts[frame + time_tap, row_tap * width : row_tap * width + area, :]
                at = 3 * time_tap + row_tap
                total = total + jnp.dot(window, w_ref[at], preferred_element_type=F32)
                if frame == 0:
                    turn_taps(w_ref, turned_ref, at)
        out_ref[rows, :] = (total * kept(length_ref, 2 * me + frame)).astype(BF16)


def back_body(area, width, total_clips, length_ref, own, cot, later, wt_ref, gin_ref, grads):
    me = lax.axis_index("tm")
    height = area // width
    for frame in range(2):
        rows = slice(frame * area, (frame + 1) * area)
        for at, ref in ((frame, cot), (2 + frame, later)):
            value = ref[rows, :].astype(F32) * kept(length_ref, 2 * me + at)
            fill_padded(grads, at, value, width, height, -1)
    for frame in range(2):
        rows = slice(frame * area, (frame + 1) * area)
        total = jnp.zeros((area, gin_ref.shape[1]), F32)
        for time_tap in range(3):
            for row_tap in range(3):
                first = (2 - row_tap) * width
                window = grads[frame + 2 - time_tap, first : first + area, :]
                total = total + jnp.dot(
                    window, wt_ref[3 * time_tap + row_tap], preferred_element_type=F32
                )
        values = own[rows, :].astype(F32)
        sig = jax.nn.sigmoid(values)
        slope = sig * (1.0 + values * (1.0 - sig))
        keep = kept(length_ref, 2 * me + frame)
        gin_ref[rows, :] = (total * slope * (keep / total_clips)).astype(BF16)


def local(video_clips, cotangent, weight, lengths):
    clip_count, frame_count, height, width, channels = video_clips.shape
    peers, shards = lax.axis_size("tm"), lax.axis_size("dp")
    total_clips = clip_count * shards
    area = height * width
    assert clip_count == 1 and frame_count == 2, "block shape"
    assert 2 * channels == peers * LANES and peers == 4, "tm size"
    clips = video_clips.reshape(2 * area, channels)
    cot = cotangent.reshape(2 * area, channels)

    block = (2 * area, channels)
    near_a = cross(clips, True)
    near_b = cross(clips, False)
    *slices, own = call(
        functools.partial(slice_body, peers, area),
        [pltpu.VMEM((area, LANES), BF16)] * peers + [pltpu.VMEM(block, BF16)],
        (cot, clips),
        resident=False,
        scratch=[
            pltpu.VMEM((channels // LANES, 2 * area, LANES), BF16),
            pltpu.VMEM((peers, area, LANES), F32),
            pltpu.SemaphoreType.DMA((channels // LANES + 1,)),
        ],
    )
    slices[1] = cross(slices[1], True)
    slices[2] = cross(slices[2], False)
    slices[3] = swap(slices[3], "tm", 3)
    split = area + area // 8
    relayed = [
        call(functools.partial(cut_body, start), [pltpu.VMEM((size, channels), BF16)], (near,))[0]
        for start, size, near in ((0, split, near_a), (split, 2 * area - split, near_b))
    ]
    first = cross(relayed[0], False)
    second = cross(relayed[1], True)
    later = lax.ppermute(cot, "tm", [(s, s - 1) for s in range(1, peers)])
    moved = pltpu.VMEM((2 * (peers + 1) * area, 5 * LANES), BF16)
    turned_acts = pltpu.VMEM((channels, 6 * area), BF16)
    act_t, grads = call(
        functools.partial(own_body, area, width), [turned_acts, moved], (lengths, own, slices[0])
    )
    parts = shards // 2
    count = channels // shards
    grads, act_t = call(
        functools.partial(near_body, area, width),
        [moved, turned_acts],
        (lengths, slices[1], near_a, near_b, grads, act_t),
        aliases={4: 0, 5: 1},
    )
    grads, *products = call(
        functools.partial(products_body, area, width),
        [moved] + [pltpu.VMEM((channels, 5 * LANES), F32)] * 3,
        (lengths, slices[2], slices[3], act_t, grads),
        aliases={4: 0},
        flops=2 * 27 * 2 * peers * area * channels * LANES // 2,
    )
    half = 27 * 2 * area * channels * LANES // 2
    send, last_turned = call(
        functools.partial(send_body, count, area),
        [pltpu.VMEM(sums_shape(parts, count), BF16), pltpu.VMEM((channels, 2 * area), BF16)],
        (grads, first, second, *products),
        flops=half,
    )
    (keep,) = call(
        functools.partial(keep_body, count, area),
        [pltpu.VMEM(sums_shape(parts, count), F32)],
        (grads, last_turned, *products),
        after=(send,),
        flops=half,
    )
    flat = weight.reshape(9, 3 * channels, channels)
    token = pltpu.VMEM((8, LANES), F32)
    padded = pltpu.VMEM((4, area + 2 * width, 3 * channels), BF16)
    flops = 2 * 27 * 2 * area * channels * channels
    conv_out, token_a, turned = call(
        functools.partial(ahead_body, area, width),
        [sds(block, BF16), token, pltpu.VMEM(flat.shape, BF16)],
        (lengths, own, near_a, near_b, first, second, flat),
        after=(keep,),
        scratch=[padded],
        flops=flops,
    )
    piece = sum_over_clips(keep, send, (token_a,))
    (input_grad,) = call(
        functools.partial(back_body, area, width, total_clips),
        [sds(block, BF16)],
        (lengths, own, cot, later, turned),
        after=(piece,),
        scratch=[padded],
        flops=flops,
    )
    pieces = [piece] + swaps([piece] * (peers - 1), "tm", 1)
    (placed,) = call(
        functools.partial(place_body, peers, 1.0 / total_clips),
        [sds((27, count, channels), F32)],
        pieces,
        scratch=[
            pltpu.VMEM((peers, *piece.shape), BF16),
            pltpu.VMEM((27, count, channels), F32),
            pltpu.SemaphoreType.DMA((9,)),
        ],
        out_space=pl.ANY,
    )
    shape = video_clips.shape
    weight_grad = placed.reshape(3, 3, 3, count, channels)
    return conv_out.reshape(shape), input_grad.reshape(shape), weight_grad


def cuts(parts):
    found = []
    while parts > 1:
        if parts % 4 == 0:
            found.append(parts)
        parts //= 4 if parts % 4 == 0 else 2
    return found


def solution(mesh):
    in_specs = (P("dp", "tm", None, None, None), P("dp", "tm", None, None, None), P(), P("dp"))
    out_specs = (
        P("dp", "tm", None, None, None),
        P("dp", "tm", None, None, None),
        P(None, None, None, "dp", None),
    )

    program = jax.shard_map(local, mesh=mesh, in_specs=in_specs, out_specs=out_specs, check_vma=False)
    sizes = cuts(mesh.shape["dp"] // 2)
    assert sizes, "dp size"
    return program
```
